32 devices in a mesh: dp: 8 (over z, x), ctx: 4 (over y, core).
Axes of the slice: x: 2, y: 2, z: 4, core: 2. Of those that a mesh axis runs over, the one named last changes fastest.
Arguments:
- tokens: bfloat16 [16, 2048, 768], P('dp', 'ctx'), may hold values from -6 to 6
- segments: int32 [16, 2048], P('dp'), may hold values from 0 to 4, never falling along the last dimension, each value on 1 to 800 neighbouring positions
- cotangent: bfloat16 [16, 2048, 768], P('dp', 'ctx'), may hold values from -6 to 6
- query_weight: bfloat16 [768, 768], P(('dp', 'ctx')), may hold values from -0.21875 to 0.21875
- query_bias: bfloat16 [768], P(('dp', 'ctx')), may hold values from -3 to 3
- key_weight: bfloat16 [768, 768], P(('dp', 'ctx')), may hold values from -0.21875 to 0.21875
- value_weight: bfloat16 [768, 768], P(('dp', 'ctx')), may hold values from -0.21875 to 0.21875
- value_bias: bfloat16 [768], P(('dp', 'ctx')), may hold values from -0.59765625 to 0.59765625
- output_weight: bfloat16 [768, 768], P(('dp', 'ctx')), may hold values from -0.875 to 0.875
- output_bias: bfloat16 [768], P(('dp', 'ctx')), may hold values from -2 to 2
- first_gain: bfloat16 [768], P(('dp', 'ctx')), may hold values from 0.5 to 1.5
- first_shift: bfloat16 [768], P(('dp', 'ctx')), may hold values from -2 to 2
- inner_weight: bfloat16 [768, 3072], P(('dp', 'ctx')), may hold values from -0.21875 to 0.21875
- inner_bias: bfloat16 [3072], P(('dp', 'ctx')), may hold values from -3 to 3
- outer_weight: bfloat16 [3072, 768], P(('dp', 'ctx')), may hold values from -0.109375 to 0.109375
- outer_bias: bfloat16 [768], P(('dp', 'ctx')), may hold values from -2 to 2
- second_gain: bfloat16 [768], P(('dp', 'ctx')), may hold values from 0.5 to 1.5
- second_shift: bfloat16 [768], P(('dp', 'ctx')), may hold values from -2 to 2
Outputs:
- layer_output: bfloat16 [16, 2048, 768], P('dp', 'ctx')
- input_gradient: float32 [16, 2048, 768], P('dp', 'ctx')
- query_weight_gradient: float32 [768, 768], P(('dp', 'ctx'))
- query_bias_gradient: float32 [768], P(('dp', 'ctx'))
- key_weight_gradient: float32 [768, 768], P(('dp', 'ctx'))
- value_weight_gradient: float32 [768, 768], P(('dp', 'ctx'))
- value_bias_gradient: float32 [768], P(('dp', 'ctx'))
- output_weight_gradient: float32 [768, 768], P(('dp', 'ctx'))
- output_bias_gradient: float32 [768], P(('dp', 'ctx'))
- first_gain_gradient: float32 [768], P(('dp', 'ctx'))
- first_shift_gradient: float32 [768], P(('dp', 'ctx'))
- inner_weight_gradient: float32 [768, 3072], P(('dp', 'ctx'))
- inner_bias_gradient: float32 [3072], P(('dp', 'ctx'))
- outer_weight_gradient: float32 [3072, 768], P(('dp', 'ctx'))
- outer_bias_gradient: float32 [768], P(('dp', 'ctx'))
- second_gain_gradient: float32 [768], P(('dp', 'ctx'))
- second_shift_gradient: float32 [768], P(('dp', 'ctx'))
The draws below stay inside these ranges and needn't reach their ends.
Inputs may be any that keep to these rules, and one draw needn't show every extreme that they name: `segments`: in each sequence the document numbers start at 0 and never fall; a document has 1 to 800 tokens, one of each sequence exactly 800, and there are at most 5 documents.
All inputs are finite; a program needn't handle non-finite values.
Results may differ from the reference program's by a relative error of at most 0.028.
Values may be sent and summed in bfloat16 or wider, within the bound.
No kernel may reach another device: no remote copies, remote signals or barrier semaphores. Data moves between devices by JAX's collectives and lax.ppermute only.
A program may use at most 384 MiB of HBM per device.

```python
import math
import jax
import jax.numpy as jnp
import numpy as np
from jax import lax

D = 768
HEADS = 12
HEAD = 64
FF = 3072
SEQ = 2048
DOCS = 5
DOC_MOST = 800
SEQS = 16


def raised(values, own_key, source, target, shards_of, factor):
    owner, partner = [(jnp.arange(values.shape[position]) // (values.shape[position] // shards_of)).reshape([-1 if axis == position else 1 for axis in range(values.ndim)]) for position in (source, target)]
    chosen = jax.random.permutation(own_key, shards_of)[partner]
    strong = (owner == chosen) | (owner == (partner + shards_of // 2) % shards_of)
    return jnp.where(strong, factor * values, values)


def level_of(stream_key, dims, cuts, low, top_value):
    def one(position, blocks):
        heights = jax.random.uniform(jax.random.fold_in(jax.random.fold_in(stream_key, 6), position), (blocks,), jnp.float32, low / len(cuts), top_value / len(cuts))
        return jnp.repeat(jnp.exp(heights), dims[position] // blocks).reshape((-1,) + (1,) * (len(dims) - position - 1))

    loudness = one(*cuts[0])
    for cut in cuts[1:]:
        loudness = loudness * one(*cut)
    return loudness


def split_up(count, total, limit, skew):
    portions = [(1 << 20) // math.isqrt(grade ** skew) + 1 for grade in range(2, count + 1)]
    surplus, counts = total - limit - (count - 1), [1] * (count - 1)
    while surplus > 0:
        free = [i for i in range(count - 1) if counts[i] < limit]
        mass, remaining = sum([portions[i] for i in free]), surplus
        for i in free:
            more = min(limit - counts[i], max(1, remaining * portions[i] // mass), surplus)
            counts[i] = counts[i] + more
            surplus = surplus - more
    return np.array([limit] + counts)


def ragged(own_key, amount, total, limit, lean):
    if amount == 2:
        one = jax.random.randint(own_key, (), max(1, total - limit), min(limit, total - 1) + 1)
        return jnp.stack([one, total - one])
    sizes = jnp.asarray(split_up(amount, total, limit, lean), jnp.int32)
    twos = (amount - 1) // 2
    source_of, sink = sizes[1:1 + 2 * twos:2], sizes[2:2 + 2 * twos:2]
    room = jnp.minimum(source_of - 1, limit - sink)
    shifted = jax.random.randint(jax.random.fold_in(own_key, 1), (twos,), 0, 1 << 20) % (room + 1)
    sizes = sizes.at[1:1 + 2 * twos:2].set(source_of - shifted).at[2:2 + 2 * twos:2].set(sink + shifted)
    return sizes[jax.random.permutation(jax.random.fold_in(own_key, 2), amount)]


def scatter_about(rng, shape, scale, reach, cuts=(), dtype=jnp.bfloat16):
    entries = scale * jax.random.normal(rng, shape, jnp.float32)
    if cuts:
        entries = entries * level_of(rng, shape, cuts, -0.22, 0.18)
    return jnp.clip(entries, -reach, reach).astype(dtype)


def heavy_noise(rng, shape, scale, reach, shards, heavy, dtype=jnp.bfloat16):
    array = scale * jax.random.normal(rng, shape, jnp.float32)
    if shards:
        array = array * level_of(rng, shape, shards, -0.22, 0.18)
    return jnp.clip(raised(array, jax.random.fold_in(rng, 3), *heavy), -reach, reach).astype(dtype)


def setup_inputs(seed: int = 0) -> dict:
    splits = jax.random.split(jax.random.key(seed), 19)
    return {
        "tokens": scatter_about(splits[0], (SEQS, SEQ, D), 1.0, 6.0, ((0, 8), (1, 4))),
        "segments": jax.vmap(lambda own: jnp.searchsorted(jnp.cumsum(ragged(own, DOCS, SEQ, DOC_MOST, 0)), jnp.arange(SEQ), side="right"))(jax.random.split(splits[1], SEQS)).reshape((SEQS, SEQ)).astype(jnp.int32),
        "cotangent": heavy_noise(splits[2], (SEQS, SEQ, D), 1.0, 6.0, ((0, 8), (1, 4)), (0, 2, 8, 2.0)),
        "query_weight": scatter_about(splits[3], (D, D), D ** -0.5, 0.21875, ((0, 32),)),
        "query_bias": scatter_about(splits[4], (D,), 0.5, 3.0, ((0, 32),)),
        "key_weight": scatter_about(splits[5], (D, D), D ** -0.5, 0.21875, ((0, 32),)),
        "value_weight": scatter_about(splits[6], (D, D), D ** -0.5, 0.21875, ((0, 32),)),
        "value_bias": scatter_about(splits[7], (D,), 0.1, 0.59765625, ((0, 32),)),
        "output_weight": scatter_about(splits[8], (D, D), (D // 16) ** -0.5, 0.875, ((0, 32),)),
        "output_bias": scatter_about(splits[9], (D,), 0.3, 2.0, ((0, 32),)),
        "first_gain": jnp.clip(1.0 + 0.1 * jax.random.normal(splits[10], (D,), jnp.float32), 0.5, 1.5).astype(jnp.bfloat16),
        "first_shift": scatter_about(splits[11], (D,), 0.3, 2.0, ((0, 32),)),
        "inner_weight": scatter_about(splits[12], (D, FF), D ** -0.5, 0.21875, ((0, 32),)),
        "inner_bias": scatter_about(splits[13], (FF,), 0.5, 3.0, ((0, 32),)),
        "outer_weight": scatter_about(splits[14], (FF, D), FF ** -0.5, 0.109375, ((0, 32),)),
        "outer_bias": scatter_about(splits[15], (D,), 0.3, 2.0, ((0, 32),)),
        "second_gain": jnp.clip(1.0 + 0.1 * jax.random.normal(splits[16], (D,), jnp.float32), 0.5, 1.5).astype(jnp.bfloat16),
        "second_shift": scatter_about(splits[17], (D,), 0.3, 2.0, ((0, 32),)),
    }


epsilon = 1e-05
highest = lax.Precision.HIGHEST

@jax.custom_vjp
def low(v):
    return lax.optimization_barrier(v.astype(jnp.bfloat16)).astype(jnp.float32)

@jax.custom_vjp
def low_back(v):
    return v

def low_keep(v):
    return (low(v), None)

def low_pass(kept, grad):
    return (grad,)

def back_keep(v):
    return (v, None)

def back_low(kept, grad):
    return (low(grad),)
low.defvjp(low_keep, low_pass)
low_back.defvjp(back_keep, back_low)

def rounded_both(values):
    return low(low_back(values))

def product(left, right):
    return jnp.dot(left, right, precision=highest)

def layer_norm(values, gain, shift):
    average = lax.optimization_barrier(jnp.mean(values, axis=-1, keepdims=True))
    centred = values - average
    spread = lax.optimization_barrier(jnp.mean(centred * centred, axis=-1, keepdims=True))
    return centred * lax.rsqrt(spread + epsilon) * gain + shift

def attend(query_piece, keys, values, query_segments, key_segments, scale):
    scores = low_back(jnp.einsum('qhd,khd->hqk', query_piece, keys, precision=highest) * scale)
    allowed = query_segments[None, :, None] == key_segments[None, None, :]
    masked = jnp.where(allowed, scores, -1e+30)
    largest = lax.optimization_barrier(jnp.max(masked, axis=-1, keepdims=True))
    logsum = largest + jnp.log(lax.optimization_barrier(jnp.sum(jnp.exp(masked - largest), axis=-1, keepdims=True)))
    probs = jnp.exp(masked - logsum)
    return jnp.einsum('hqk,khd->qhd', low(probs), values, precision=highest)

def sequence_forward(source, seg_row, weights):
    scale = 1.0 / math.sqrt(HEAD)
    queries = rounded_both(product(source, weights[0]) + weights[1]).reshape(SEQ, HEADS, HEAD)
    keys = rounded_both(product(source, weights[2])).reshape(SEQ, HEADS, HEAD)
    values = rounded_both(product(source, weights[3]) + weights[4]).reshape(SEQ, HEADS, HEAD)
    block = min(512, SEQ)
    count = SEQ // block

    def one_block(pieces):
        query_piece, seg_piece = pieces
        return attend(query_piece, keys, values, seg_piece, seg_row, scale)
    mixed = lax.map(jax.checkpoint(one_block), (queries.reshape(count, block, HEADS, HEAD), seg_row.reshape(count, block)))
    mixed = rounded_both(mixed.reshape(SEQ, D))
    pre = source + low_back(product(mixed, weights[5]) + weights[6])
    first = layer_norm(pre, weights[7], weights[8])
    inner = low_back(product(low(first), weights[9]) + weights[10])
    active = low(jax.nn.gelu(inner, approximate=False))
    total = first + low_back(product(active, weights[11]) + weights[12])
    return layer_norm(total, weights[13], weights[14])

def reference(tokens, segments, cotangent, query_weight, query_bias, key_weight, value_weight, value_bias, output_weight, output_bias, first_gain, first_shift, inner_weight, inner_bias, outer_weight, outer_bias, second_gain, second_shift):
    params = jax.tree.map(lambda weight: weight.astype(jnp.float32), (query_weight, query_bias, key_weight, value_weight, value_bias, output_weight, output_bias, first_gain, first_shift, inner_weight, inner_bias, outer_weight, outer_bias, second_gain, second_shift))

    def one_sequence(totals, pieces):
        source, seg_row, upstream = pieces
        result, pullback = jax.vjp(lambda inputs, weights: sequence_forward(inputs, seg_row, weights), source.astype(jnp.float32), params)
        d_input, d_params = pullback(upstream.astype(jnp.float32))
        return (jax.tree.map(jnp.add, totals, d_params), (result.astype(jnp.bfloat16), d_input))
    zeros = jax.tree.map(jnp.zeros_like, params)
    totals, outputs = lax.scan(one_sequence, zeros, (tokens, segments, cotangent))
    return (outputs[0], outputs[1], totals[0], totals[1], totals[2], totals[3], totals[4], totals[5], totals[6], totals[7], totals[8], totals[9], totals[10], totals[11], totals[12], totals[13], totals[14])
```

```python
import math

import jax
import jax.numpy as jnp
from jax import lax
from jax.experimental import pallas as pl
from jax.experimental.pallas import tpu as pltpu
from jax.sharding import Mesh
from jax.sharding import PartitionSpec as P

HEAD = 64
PAIR = 2 * HEAD
BLOCK = 256
LOG2E = math.log2(math.e)
epsilon = 1e-05
f32 = jnp.float32
bf16 = jnp.bfloat16


def dot(left, right):
    return jnp.dot(left, right, preferred_element_type=f32)


def lanes_of(shape, head):
    lane = lax.broadcasted_iota(jnp.int32, shape, 1)
    return (lane < HEAD) if head == 0 else (lane >= HEAD)


def rows_of(shape, head):
    row = lax.broadcasted_iota(jnp.int32, shape, 0)
    return (row < HEAD) if head == 0 else (row >= HEAD)


def attend_kernel(lo, hi, q_ref, k_ref, v_ref, seg_col_ref, seg_row_ref, o_ref, lse_ref, kt_ref, v0_ref, v1_ref):
    step = pl.program_id(0)

    @pl.when(step == 0)
    def _():
        kt_ref[...] = k_ref[...].astype(f32).T.astype(bf16)
        values = v_ref[...].astype(f32)
        v0_ref[...] = jnp.where(lanes_of(values.shape, 0), values, 1.0).astype(bf16)
        v1_ref[...] = jnp.where(lanes_of(values.shape, 1), values, 1.0).astype(bf16)

    queries = q_ref[...].astype(f32)
    split = [jnp.where(lanes_of(queries.shape, h), queries, 0.0).astype(bf16) for h in (0, 1)]
    seg_q = seg_col_ref[:, 0:1]
    values_of = (v0_ref, v1_ref)

    def one(block, carry):
        at = pl.multiple_of(block * BLOCK, BLOCK)
        keys_t = kt_ref[:, pl.ds(at, BLOCK)]
        allowed = seg_q == seg_row_ref[0:1, pl.ds(at, BLOCK)]
        out = []
        for h in (0, 1):
            peak, acc = carry[2 * h], carry[2 * h + 1]
            scores = jnp.where(allowed, dot(split[h], keys_t) * (LOG2E / math.sqrt(HEAD)), -1e30)
            top = jnp.maximum(peak, jnp.max(scores, axis=1, keepdims=True))
            probs = jnp.exp2(scores - top)
            acc = acc * jnp.exp2(peak - top) + dot(probs.astype(bf16), values_of[h][pl.ds(at, BLOCK), :])
            out += [top, acc]
        return tuple(out)

    start = (jnp.full((BLOCK, 1), -1e30, f32), jnp.zeros((BLOCK, PAIR), f32)) * 2
    peak0, acc0, peak1, acc1 = lax.fori_loop(lo[step], hi[step], one, start)
    sums0 = pltpu.roll(acc0, HEAD, 1)
    sums1 = pltpu.roll(acc1, HEAD, 1)
    first = lanes_of(acc0.shape, 0)
    o_ref[...] = (jnp.where(first, acc0, acc1) / jnp.where(first, sums0, sums1)).astype(bf16)
    logs = jnp.where(first, peak1 + jnp.log2(acc1), peak0 + jnp.log2(acc0)).T
    lse_ref[0, 0:8, :] = logs[HEAD : HEAD + 8, :]
    lse_ref[0, 8:16, :] = logs[0:8, :]


def attend_back_kernel(
    lo, hi, q_ref, k_ref, v_ref, do_ref, o_ref, lse_ref, seg_row_ref, seg_col_ref,
    dq_ref, dk_ref, dv_ref, kt_ref, dk_acc, dv_acc,
):
    step = pl.program_id(0)

    @pl.when(step == 0)
    def _():
        kt_ref[...] = k_ref[...].astype(f32).T.astype(bf16)
        dk_acc[...] = jnp.zeros_like(dk_acc)
        dv_acc[...] = jnp.zeros_like(dv_acc)

    queries = q_ref[...].astype(f32)
    grads = do_ref[...].astype(f32)
    queries_t = queries.T
    grads_t = grads.T
    inner_t = grads_t * o_ref[...].astype(f32).T
    q_rows = [jnp.where(lanes_of(queries.shape, h), queries, 0.0).astype(bf16) for h in (0, 1)]
    g_rows = [jnp.where(lanes_of(grads.shape, h), grads, 0.0).astype(bf16) for h in (0, 1)]
    q_cols = [jnp.where(rows_of(queries_t.shape, h), queries_t, 0.0).astype(bf16) for h in (0, 1)]
    g_cols = [jnp.where(rows_of(grads_t.shape, h), grads_t, 0.0).astype(bf16) for h in (0, 1)]
    mean = [jnp.sum(inner_t[h * HEAD : (h + 1) * HEAD, :], axis=0, keepdims=True) for h in (0, 1)]
    logs = [lse_ref[0, 8 * h : 8 * h + 1, :] for h in (0, 1)]
    seg_q = seg_row_ref[0:1, :]

    def one(block, carry):
        at = pl.multiple_of(block * BLOCK, BLOCK)
        keys = k_ref[pl.ds(at, BLOCK), :]
        values = v_ref[pl.ds(at, BLOCK), :]
        allowed = seg_col_ref[pl.ds(at, BLOCK), 0:1] == seg_q
        probs, scores_grad, out = [], [], []
        for h in (0, 1):
            scores = dot(keys, q_cols[h]) * (LOG2E / math.sqrt(HEAD)) - logs[h]
            p = jnp.exp2(jnp.where(allowed, scores, -1e30))
            ds = (p * (dot(values, g_cols[h]) - mean[h])).astype(bf16)
            probs.append(p.astype(bf16))
            scores_grad.append(ds)
            out.append(carry[h] + dot(kt_ref[h * HEAD : (h + 1) * HEAD, pl.ds(at, BLOCK)], ds))
        dv_acc[pl.ds(at, BLOCK), :] += dot(probs[0], g_rows[0]) + dot(probs[1], g_rows[1])
        dk_acc[pl.ds(at, BLOCK), :] += dot(scores_grad[0], q_rows[0]) + dot(scores_grad[1], q_rows[1])
        return tuple(out)

    start = (jnp.zeros((HEAD, BLOCK), f32),) * 2
    dq0, dq1 = lax.fori_loop(lo[step], hi[step], one, start)
    dq_ref[...] = (jnp.concatenate([dq0, dq1], axis=0).T * (1.0 / math.sqrt(HEAD))).astype(bf16)

    @pl.when(step == pl.num_programs(0) - 1)
    def _():
        dk_ref[...] = (dk_acc[...] * (1.0 / math.sqrt(HEAD))).astype(bf16)
        dv_ref[...] = dv_acc[...].astype(bf16)


def key_range(seg):
    blocks = seg.reshape(-1, BLOCK)
    first = jnp.sum(seg[None, :] < blocks[:, :1], axis=1, dtype=jnp.int32)
    last = jnp.sum(seg[None, :] <= blocks[:, -1:], axis=1, dtype=jnp.int32)
    return first // BLOCK, (last + BLOCK - 1) // BLOCK


def attend(qkv, pair, pairs, seg_row, seg_col, lo, hi):
    length = qkv.shape[0]
    whole = lambda part: pl.BlockSpec((length, PAIR), lambda i, lo, hi: (0, part * pairs + pair))
    return pl.pallas_call(
        attend_kernel,
        out_shape=(
            jax.ShapeDtypeStruct((length, PAIR), bf16),
            jax.ShapeDtypeStruct((1, 16, length), f32),
        ),
        grid_spec=pltpu.PrefetchScalarGridSpec(
            num_scalar_prefetch=2,
            grid=(length // BLOCK,),
            in_specs=[
                pl.BlockSpec((BLOCK, PAIR), lambda i, lo, hi: (i, pair)),
                whole(1),
                whole(2),
                pl.BlockSpec((BLOCK, PAIR), lambda i, lo, hi: (i, 0)),
                pl.BlockSpec((8, length), lambda i, lo, hi: (0, 0)),
            ],
            out_specs=[
                pl.BlockSpec((BLOCK, PAIR), lambda i, lo, hi: (i, 0)),
                pl.BlockSpec((1, 16, BLOCK), lambda i, lo, hi: (0, 0, i)),
            ],
            scratch_shapes=[
                pltpu.VMEM((PAIR, length), bf16),
                pltpu.VMEM((length, PAIR), bf16),
                pltpu.VMEM((length, PAIR), bf16),
            ],
        ),
        compiler_params=pltpu.CompilerParams(dimension_semantics=("arbitrary",)),
        name="attend",
    )(lo, hi, qkv, qkv, qkv, seg_col, seg_row)


def attend_back(qkv, pair, pairs, mixed, d_mixed, lse, seg_row, seg_col, lo, hi):
    length = qkv.shape[0]
    whole = lambda part: pl.BlockSpec((length, PAIR), lambda i, lo, hi: (0, part * pairs + pair))
    rows = pl.BlockSpec((BLOCK, PAIR), lambda i, lo, hi: (i, 0))
    out = pl.BlockSpec((length, PAIR), lambda i, lo, hi: (0, 0))
    half = jax.ShapeDtypeStruct((length, PAIR), bf16)
    return pl.pallas_call(
        attend_back_kernel,
        out_shape=(half, half, half),
        grid_spec=pltpu.PrefetchScalarGridSpec(
            num_scalar_prefetch=2,
            grid=(length // BLOCK,),
            in_specs=[
                pl.BlockSpec((BLOCK, PAIR), lambda i, lo, hi: (i, pair)),
                whole(1),
                whole(2),
                pl.BlockSpec((BLOCK, PAIR), lambda i, lo, hi: (i, pair)),
                rows,
                pl.BlockSpec((1, 16, BLOCK), lambda i, lo, hi: (0, 0, i)),
                pl.BlockSpec((8, BLOCK), lambda i, lo, hi: (0, i)),
                pl.BlockSpec((length, PAIR), lambda i, lo, hi: (0, 0)),
            ],
            out_specs=[rows, out, out],
            scratch_shapes=[
                pltpu.VMEM((PAIR, length), bf16),
                pltpu.VMEM((length, PAIR), f32),
                pltpu.VMEM((length, PAIR), f32),
            ],
        ),
        compiler_params=pltpu.CompilerParams(dimension_semantics=("arbitrary",)),
        name="attend_back",
    )(lo, hi, qkv, qkv, qkv, d_mixed, mixed, lse, seg_row, seg_col)


def bit_of(name):
    axis, step = name
    return (lax.axis_index(axis) // step) % 2


def swap(values, name):
    axis, step = name
    count = lax.axis_size(axis)
    return lax.ppermute(values, axis, [(i, i ^ step) for i in range(count)])


def pick(values, index, dim):
    return lax.dynamic_index_in_dim(values, index, dim, keepdims=False)


def in_order(bit, mine, other, dim=0):
    low = jnp.where(bit == 0, mine, other)
    high = jnp.where(bit == 0, other, mine)
    return jnp.stack([low, high], axis=dim)


def grow(values, names):
    for name in names:
        values = in_order(bit_of(name), values, swap(values, name))
    return values


def sort_blocks(values, names, wanted):
    stacked = list(reversed(names))
    order = [stacked.index(name) for name in wanted]
    count = len(names)
    return values.transpose(order + list(range(count, values.ndim)))


def shrink(values, names, wanted):
    left = list(wanted)
    for name in names:
        dim = left.index(name)
        bit = bit_of(name)
        got = swap(pick(values, 1 - bit, dim), name)
        values = pick(values, bit, dim).astype(f32) + got.astype(f32)
        left.remove(name)
        if left:
            values = values.astype(bf16)
    return values


def norm_stats(values):
    average = jnp.mean(values, axis=-1, keepdims=True)
    centred = values - average
    spread = jnp.mean(centred * centred, axis=-1, keepdims=True)
    inverse = lax.rsqrt(spread + epsilon)
    return centred * inverse, inverse


def norm_back(grad, gain, unit, inverse):
    u = grad * gain
    first = jnp.mean(u, axis=-1, keepdims=True)
    second = jnp.mean(u * unit, axis=-1, keepdims=True)
    return (u - first - unit * second) * inverse


def dot_rows(left, right):
    return lax.dot_general(left, right, (((0,), (0,)), ((), ())), preferred_element_type=f32)


def dot_cols(left, right):
    return lax.dot_general(left, right, (((1,), (1,)), ((), ())), preferred_element_type=f32)


def column_sums(values):
    return jnp.sum(values.astype(f32), axis=0)


def on_device(
    tokens, segments, cotangent, query_weight, query_bias, key_weight, value_weight, value_bias,
    output_weight, output_bias, first_gain, first_shift, inner_weight, inner_bias, outer_weight,
    outer_bias, second_gain, second_shift,
):
    core = ("c", 1)
    partner = ("y", 1)
    y = bit_of(partner)
    c = bit_of(core)
    local, width = tokens.shape[1], tokens.shape[2]
    own, hidden = inner_weight.shape
    half = width // 2
    pairs = half // PAIR
    length = segments.shape[1]
    chunks = hidden // width
    bits = lambda axis: [(axis, 1 << k) for k in reversed(range(lax.axis_size(axis).bit_length() - 1))]
    y_names = bits("y")
    far, near = bits("dp")[:-1], bits("dp")[-1]
    wanted = bits("dp") + y_names
    team = y_names[:-1]
    rank = lax.axis_index("y") // 2
    blocks = (2,) * len(wanted)

    columns = jnp.stack(
        [query_bias, value_bias, output_bias, first_gain, first_shift, outer_bias, second_gain, second_shift],
        axis=1,
    )
    columns = jnp.concatenate([columns, inner_bias.reshape(own, chunks)], axis=1)
    columns = jnp.pad(columns, ((0, 0), (0, PAIR - columns.shape[1])))

    def three(index):
        return jnp.concatenate(
            [lax.dynamic_slice_in_dim(w, index * half, half, 1) for w in (query_weight, key_weight, value_weight)]
            + [columns],
            axis=1,
        )

    attention_part = in_order(c, three(c), swap(three(1 - c), core)).reshape(2 * own, 3 * half + PAIR)

    def to_chip(values):
        return in_order(y, pick(values, y, 0), swap(pick(values, 1 - y, 0), partner))

    mine = to_chip(tokens)
    source_all = grow(in_order(c, mine, swap(mine, core), 1), team).reshape(length, width)
    source = mine.reshape(2 * local, width)

    attention_part = grow(attention_part, far)
    cut = (3 * half + PAIR) // 2 // 128 * 128
    output_inner = jnp.concatenate([output_weight, inner_weight], axis=1)
    output_inner, outer_part, attention_part = lax.optimization_barrier((output_inner, outer_weight, attention_part))
    part_a = grow(attention_part[..., :cut], [near] + y_names)
    part_b = grow(attention_part[..., cut:], y_names + [near])
    part_a = sort_blocks(part_a, far + [near] + y_names, wanted).reshape(width, cut)
    part_b = sort_blocks(part_b, far + y_names + [near], wanted).reshape(width, 3 * half + PAIR - cut)
    joined = jnp.concatenate([part_a, part_b], axis=1)
    qkv_weight = joined[:, : 3 * half]
    vectors = joined[:, 3 * half :].astype(f32).T
    half_of = lambda row: lax.dynamic_slice_in_dim(row, c * half, half, 0)
    qkv_bias = jnp.concatenate([half_of(vectors[0]), jnp.zeros((half,), f32), half_of(vectors[1])])
    output_bias, first_gain, first_shift, outer_bias, second_gain, second_shift = [vectors[k] for k in range(2, 8)]
    inner_bias = joined[:, 3 * half + 8 : 3 * half + 8 + chunks].reshape(hidden).astype(f32)

    output_inner = grow(output_inner, far)
    outer_part = grow(outer_part, far)
    output_inner = sort_blocks(grow(output_inner, [near] + y_names), far + [near] + y_names, wanted)
    outer_part = sort_blocks(grow(outer_part, y_names + [near]), far + y_names + [near], wanted)
    output_inner = in_order(c, output_inner, swap(output_inner, core), len(wanted)).reshape(width, width + hidden)
    outer_weight = in_order(c, outer_part, swap(outer_part, core), len(wanted)).reshape(hidden, width)
    output_weight = output_inner[:, :width]
    inner_weight = output_inner[:, width:]

    seg = pick(segments, y, 0)
    lo, hi = key_range(seg)
    seg_row = jnp.broadcast_to(seg[None, :], (8, length))
    seg_col = jnp.broadcast_to(seg[:, None], (length, PAIR))
    qkv = (dot(source_all, qkv_weight) + qkv_bias).astype(bf16)
    attended = [attend(qkv, p, pairs, seg_row, seg_col, lo, hi) for p in range(pairs)]
    mixed_heads = jnp.concatenate([a[0] for a in attended], axis=1)
    mixed_heads = pick(mixed_heads.reshape(-1, 2, 2, local, half), rank, 0)
    got = swap(pick(mixed_heads, 1 - c, 1), core)
    mixed = in_order(c, pick(mixed_heads, c, 1), got, 2).reshape(2 * local, width)

    pre = source.astype(f32) + dot(mixed, output_weight) + output_bias
    first_unit, first_inverse = norm_stats(pre)
    first = first_unit * first_gain + first_shift
    first_low = first.astype(bf16)
    inner = dot(first_low, inner_weight) + inner_bias
    phi = 0.5 * (1.0 + lax.erf(inner * math.sqrt(0.5)))
    active = (inner * phi).astype(bf16)
    slope = (phi + inner * (jnp.exp(-0.5 * inner * inner) * (1.0 / math.sqrt(2.0 * math.pi)))).astype(bf16)
    total = first + dot(active, outer_weight) + outer_bias
    second_unit, second_inverse = norm_stats(total)
    result = (second_unit * second_gain + second_shift).astype(bf16).reshape(2, local, width)

    def to_owner(values):
        kept = pick(values, y, 0)
        return in_order(y, kept, swap(pick(values, 1 - y, 0).astype(bf16), partner).astype(kept.dtype))

    layer_output = to_owner(result)

    grad = to_chip(cotangent).reshape(2 * local, width).astype(f32)
    d_total = norm_back(grad, second_gain, second_unit, second_inverse)
    d_second_gain = jnp.sum(grad * second_unit, axis=0)
    d_second_shift = jnp.sum(grad, axis=0)
    d_outer = d_total.astype(bf16)

    def core_then_chips(gradient, names):
        gradient = gradient.astype(bf16)
        rows, cols = gradient.shape
        shaped = gradient.reshape(blocks + (2, rows // (2 * math.prod(blocks)), cols))
        dim = len(wanted)
        got = swap(pick(shaped, 1 - c, dim), core)
        summed = (pick(shaped, c, dim).astype(f32) + got.astype(f32)).astype(bf16)
        return shrink(summed, names, wanted)

    back = list(reversed(far))
    g_outer_weight = core_then_chips(dot_rows(active, d_outer), [near] + y_names + back)
    d_inner = (dot_cols(d_outer, outer_weight) * slope.astype(f32)).astype(bf16)
    g_inner_weight = core_then_chips(dot_rows(first_low, d_inner), y_names + [near] + back)
    d_first = dot_cols(d_inner, inner_weight) + d_total
    d_pre = norm_back(d_first, first_gain, first_unit, first_inverse)
    d_attended = d_pre.astype(bf16)
    d_mixed = dot_cols(d_attended, output_weight).astype(bf16)
    d_mixed = d_mixed.reshape(2 * local, 2, half)
    got = swap(pick(d_mixed, 1 - c, 1), core)
    d_heads = in_order(c, pick(d_mixed, c, 1).reshape(2, local, half), got.reshape(2, local, half), 1)
    d_heads = grow(d_heads, reversed(team)).reshape(length, half)

    g_columns = jnp.stack(
        [
            column_sums(d_attended),
            jnp.sum(d_first * first_unit, axis=0),
            jnp.sum(d_first, axis=0),
            column_sums(d_outer),
            d_second_gain,
            d_second_shift,
        ],
        axis=1,
    )
    g_columns = jnp.concatenate([g_columns, column_sums(d_inner).reshape(width, chunks)], axis=1)
    g_columns = jnp.pad(g_columns, ((0, 0), (0, PAIR - g_columns.shape[1])))
    g_output = core_then_chips(
        jnp.concatenate([dot_rows(mixed, d_attended), g_columns], axis=1), y_names + [near] + back
    )

    grads = [
        attend_back(qkv, p, pairs, attended[p][0], d_heads, attended[p][1], seg_row, seg_col, lo, hi)
        for p in range(pairs)
    ]
    d_qkv = jnp.concatenate([g[k] for k in range(3) for g in grads], axis=1)
    place = lambda part: lax.dynamic_update_slice_in_dim(
        jnp.zeros((width,), f32), column_sums(d_qkv[:, part * half : (part + 1) * half]), c * half, 0
    )
    g_bias = jnp.pad(jnp.stack([place(0), place(2)], axis=1), ((0, 0), (0, PAIR - 2)))
    g_qkv = jnp.concatenate([dot_rows(source_all, d_qkv), g_bias], axis=1).astype(bf16)
    if team:
        g_qkv = jnp.where(rank == 0, g_qkv, jnp.zeros_like(g_qkv))
    g_qkv = g_qkv.reshape(blocks + (2 * own, 3 * half + PAIR))
    g_a = shrink(g_qkv[..., :cut], y_names + [near] + back, wanted)
    g_b = shrink(g_qkv[..., cut:], [near] + y_names + back, wanted)
    g_chip = jnp.concatenate([g_a, g_b], axis=1).reshape(2, own, 3 * half + PAIR)
    kept = pick(g_chip, c, 0)
    got = swap(pick(g_chip, 1 - c, 0), core)
    g_weights = in_order(c, kept[:, : 3 * half], got[:, : 3 * half])
    g_biases = kept[:, 3 * half :] + got[:, 3 * half :]
    g_three = [
        jnp.concatenate([g_weights[0, :, k * half : (k + 1) * half], g_weights[1, :, k * half : (k + 1) * half]], axis=1)
        for k in range(3)
    ]

    shaped = pick(d_qkv.reshape(-1, 2, 2, local, 3 * half), rank, 0)
    other = dot_cols(pick(shaped, 1 - c, 1).reshape(2 * local, 3 * half), qkv_weight).astype(bf16)
    other = swap(other, core)
    d_input = d_pre + dot_cols(pick(shaped, c, 1).reshape(2 * local, 3 * half), qkv_weight) + other.astype(f32)
    input_gradient = to_owner(d_input.reshape(2, local, width))

    return (
        layer_output,
        input_gradient,
        g_three[0],
        g_biases[:, 0],
        g_three[1],
        g_three[2],
        g_biases[:, 1],
        g_output[:, :width],
        g_output[:, width],
        g_output[:, width + 1],
        g_output[:, width + 2],
        g_inner_weight,
        g_output[:, width + 6 : width + 6 + chunks].reshape(own * chunks),
        g_outer_weight,
        g_output[:, width + 3],
        g_output[:, width + 4],
        g_output[:, width + 5],
    )


def solution(mesh):
    dp, ctx = mesh.shape["dp"], mesh.shape["ctx"]
    split = Mesh(mesh.devices.reshape(dp, ctx // 2, 2), ("dp", "y", "c"))
    every = ("dp", "y", "c")
    tokens = P("dp", ("y", "c"), None)
    matrix = P(every, None)
    vector = P(every)
    return jax.shard_map(
        on_device,
        mesh=split,
        in_specs=(
            tokens, P("dp", None), tokens,
            matrix, vector, matrix, matrix, vector, matrix, vector, vector, vector,
            matrix, vector, matrix, vector, vector, vector,
        ),
        out_specs=(
            tokens, tokens,
            matrix, vector, matrix, matrix, vector, matrix, vector, vector, vector,
            matrix, vector, matrix, vector, vector, vector,
        ),
        check_vma=False,
    )
```

```python
import functools
import math

import jax
import jax.numpy as jnp
from jax import lax
from jax.experimental import pallas as pl
from jax.experimental.pallas import tpu as pltpu
from jax.sharding import Mesh
from jax.sharding import PartitionSpec as P

from jax.sharding import Mesh
from jax.sharding import PartitionSpec as P

HEAD = 64
PAIR = 2 * HEAD
BQ = 256
BK = 256
LOG2E = math.log2(math.e)
epsilon = 1e-05
f32 = jnp.float32
bf16 = jnp.bfloat16


def dot(left, right):
    return jnp.dot(left, right, preferred_element_type=f32)


def lanes_of(shape, head):
    lane = lax.broadcasted_iota(jnp.int32, shape, 1)
    return (lane < HEAD) if head == 0 else (lane >= HEAD)


def rows_of(shape, head):
    row = lax.broadcasted_iota(jnp.int32, shape, 0)
    return (row < HEAD) if head == 0 else (row >= HEAD)


def attend_kernel(lo, hi, q_ref, k_ref, v_ref, seg_col_ref, seg_row_ref, o_ref, lse_ref, kt_ref, v_scr, *, base):
    step = pl.program_id(0)
    group = q_ref.shape[1] // PAIR
    heads = [(p, h) for p in range(group) for h in (0, 1)]
    at_pair = [slice(p * PAIR, (p + 1) * PAIR) for p in range(group)]

    @pl.when(step == 0)
    def _():
        for p in range(group):
            kt_ref[at_pair[p], :] = k_ref[:, at_pair[p]].astype(f32).T.astype(bf16)
            values = v_ref[:, at_pair[p]].astype(f32)
            for h in (0, 1):
                v_scr[2 * p + h] = jnp.where(lanes_of(values.shape, h), values, 1.0).astype(bf16)

    split = []
    for p in range(group):
        queries = q_ref[:, at_pair[p]].astype(f32)
        split += [jnp.where(lanes_of(queries.shape, h), queries, 0.0).astype(bf16) for h in (0, 1)]
    seg_q = seg_col_ref[:, 0:1]

    def one(block, carry):
        at = pl.multiple_of(block * BK, BK)
        allowed = seg_q == seg_row_ref[0:1, pl.ds(at, BK)]
        out = []
        for n, (p, h) in enumerate(heads):
            peak, acc = carry[2 * n], carry[2 * n + 1]
            scores = dot(split[n], kt_ref[at_pair[p], pl.ds(at, BK)])
            scores = jnp.where(allowed, scores * (LOG2E / math.sqrt(HEAD)), -1e30)
            top = jnp.maximum(peak, jnp.max(scores, axis=1, keepdims=True))
            probs = jnp.exp2(scores - top)
            acc = acc * jnp.exp2(peak - top) + dot(probs.astype(bf16), v_scr[n, pl.ds(at, BK), :])
            out += [top, acc]
        return tuple(out)

    start = (jnp.full((BQ, 1), -1e30, f32), jnp.zeros((BQ, PAIR), f32)) * len(heads)
    done = lax.fori_loop(lo[base + step], hi[base + step], one, start)
    for p in range(group):
        peak0, acc0, peak1, acc1 = done[4 * p : 4 * p + 4]
        sums0 = pltpu.roll(acc0, HEAD, 1)
        sums1 = pltpu.roll(acc1, HEAD, 1)
        first = lanes_of(acc0.shape, 0)
        o_ref[:, at_pair[p]] = (jnp.where(first, acc0, acc1) / jnp.where(first, sums0, sums1)).astype(bf16)
        logs = jnp.where(first, peak1 + jnp.log2(acc1), peak0 + jnp.log2(acc0)).T
        lse_ref[16 * p : 16 * p + 8, :] = logs[HEAD : HEAD + 8, :]
        lse_ref[16 * p + 8 : 16 * p + 16, :] = logs[0:8, :]


def attend_back_kernel(
    lo, hi, q_ref, k_ref, v_ref, do_ref, o_ref, lse_ref, seg_row_ref, seg_col_ref, *refs, base, last
):
    if last:
        dk_before, dv_before, dq_ref, dk_ref, dv_ref, kt_ref, dk_acc, dv_acc = refs
    else:
        dq_ref, dk_acc, dv_acc, kt_ref = refs
    step = pl.program_id(0)
    group = q_ref.shape[1] // PAIR
    at_pair = [slice(p * PAIR, (p + 1) * PAIR) for p in range(group)]

    @pl.when(step == 0)
    def _():
        for p in range(group):
            kt_ref[at_pair[p], :] = k_ref[:, at_pair[p]].astype(f32).T.astype(bf16)
        dk_acc[...] = dk_before[...] if last else jnp.zeros_like(dk_acc)
        dv_acc[...] = dv_before[...] if last else jnp.zeros_like(dv_acc)

    q_rows, g_rows, q_cols, g_cols, mean, logs = [], [], [], [], [], []
    for p in range(group):
        queries = q_ref[:, at_pair[p]].astype(f32)
        grads = do_ref[:, at_pair[p]].astype(f32)
        queries_t = queries.T
        grads_t = grads.T
        inner_t = grads_t * o_ref[:, at_pair[p]].astype(f32).T
        for h in (0, 1):
            q_rows.append(jnp.where(lanes_of(queries.shape, h), queries, 0.0).astype(bf16))
            g_rows.append(jnp.where(lanes_of(grads.shape, h), grads, 0.0).astype(bf16))
            q_cols.append(jnp.where(rows_of(queries_t.shape, h), queries_t, 0.0).astype(bf16))
            g_cols.append(jnp.where(rows_of(grads_t.shape, h), grads_t, 0.0).astype(bf16))
            mean.append(jnp.sum(inner_t[h * HEAD : (h + 1) * HEAD, :], axis=0, keepdims=True))
            logs.append(lse_ref[16 * p + 8 * h : 16 * p + 8 * h + 1, :])
    seg_q = seg_row_ref[0:1, :]

    def one(block, carry):
        at = pl.multiple_of(block * BK, BK)
        allowed = seg_col_ref[pl.ds(at, BK), 0:1] == seg_q
        out = []
        for p in range(group):
            keys = k_ref[pl.ds(at, BK), at_pair[p]]
            values = v_ref[pl.ds(at, BK), at_pair[p]]
            probs, scores_grad = [], []
            for h in (0, 1):
                n = 2 * p + h
                scores = dot(keys, q_cols[n]) * (LOG2E / math.sqrt(HEAD)) - logs[n]
                weight = jnp.exp2(jnp.where(allowed, scores, -1e30))
                ds = (weight * (dot(values, g_cols[n]) - mean[n])).astype(bf16)
                probs.append(weight.astype(bf16))
                scores_grad.append(ds)
                rows = slice(p * PAIR + h * HEAD, p * PAIR + (h + 1) * HEAD)
                out.append(carry[n] + dot(kt_ref[rows, pl.ds(at, BK)], ds))
            n = 2 * p
            dv_acc[pl.ds(at, BK), at_pair[p]] += dot(probs[0], g_rows[n]) + dot(probs[1], g_rows[n + 1])
            dk_acc[pl.ds(at, BK), at_pair[p]] += dot(scores_grad[0], q_rows[n]) + dot(scores_grad[1], q_rows[n + 1])
        return tuple(out)

    start = (jnp.zeros((HEAD, BQ), f32),) * (2 * group)
    done = lax.fori_loop(lo[base + step], hi[base + step], one, start)
    for p in range(group):
        turned = jnp.concatenate([done[2 * p], done[2 * p + 1]], axis=0).T
        dq_ref[:, at_pair[p]] = (turned * (1.0 / math.sqrt(HEAD))).astype(bf16)

    if not last:
        return

    @pl.when(step == pl.num_programs(0) - 1)
    def _():
        dk_ref[...] = (dk_acc[...] * (1.0 / math.sqrt(HEAD))).astype(bf16)
        dv_ref[...] = dv_acc[...].astype(bf16)


def key_range(seg):
    blocks = seg.reshape(-1, BQ)
    first = jnp.sum(seg[None, :] < blocks[:, :1], axis=1, dtype=jnp.int32)
    last = jnp.sum(seg[None, :] <= blocks[:, -1:], axis=1, dtype=jnp.int32)
    return first // BK, (last + BK - 1) // BK


def attend(qkv, base, count, seg_row, seg_col, lo, hi):
    length, wide = qkv.shape
    half = wide // 3
    whole = lambda part: pl.BlockSpec((length, half), lambda i, lo, hi: (0, part))
    return pl.pallas_call(
        functools.partial(attend_kernel, base=base),
        out_shape=(
            jax.ShapeDtypeStruct((count * BQ, half), bf16),
            jax.ShapeDtypeStruct((half // PAIR * 16, count * BQ), f32),
        ),
        grid_spec=pltpu.PrefetchScalarGridSpec(
            num_scalar_prefetch=2,
            grid=(count,),
            in_specs=[
                pl.BlockSpec((BQ, half), lambda i, lo, hi: (base + i, 0)),
                whole(1),
                whole(2),
                pl.BlockSpec((BQ, PAIR), lambda i, lo, hi: (base + i, 0)),
                pl.BlockSpec((8, length), lambda i, lo, hi: (0, 0)),
            ],
            out_specs=[
                pl.BlockSpec((BQ, half), lambda i, lo, hi: (i, 0)),
                pl.BlockSpec((half // PAIR * 16, BQ), lambda i, lo, hi: (0, i)),
            ],
            scratch_shapes=[
                pltpu.VMEM((half, length), bf16),
                pltpu.VMEM((half // HEAD, length, PAIR), bf16),
            ],
        ),
        compiler_params=pltpu.CompilerParams(dimension_semantics=("arbitrary",)),
        name="attend",
    )(lo, hi, qkv, qkv, qkv, seg_col, seg_row)


def attend_back(qkv, base, count, before, mixed, d_mixed, lse, seg_row, seg_col, lo, hi):
    length, wide = qkv.shape
    half = wide // 3
    whole = lambda part: pl.BlockSpec((length, half), lambda i, lo, hi: (0, part))
    rows = pl.BlockSpec((BQ, half), lambda i, lo, hi: (base + i, 0))
    last = bool(before)
    kind = bf16 if last else f32
    return pl.pallas_call(
        functools.partial(attend_back_kernel, base=base, last=last),
        out_shape=(
            jax.ShapeDtypeStruct((count * BQ, half), bf16),
            jax.ShapeDtypeStruct((length, half), kind),
            jax.ShapeDtypeStruct((length, half), kind),
        ),
        grid_spec=pltpu.PrefetchScalarGridSpec(
            num_scalar_prefetch=2,
            grid=(count,),
            in_specs=[
                rows,
                whole(1),
                whole(2),
                rows,
                rows,
                pl.BlockSpec((half // PAIR * 16, BQ), lambda i, lo, hi: (0, base + i)),
                pl.BlockSpec((8, BQ), lambda i, lo, hi: (0, base + i)),
                pl.BlockSpec((length, PAIR), lambda i, lo, hi: (0, 0)),
            ]
            + [whole(0)] * len(before),
            out_specs=[pl.BlockSpec((BQ, half), lambda i, lo, hi: (i, 0)), whole(0), whole(0)],
            scratch_shapes=[pltpu.VMEM((half, length), bf16)] + [pltpu.VMEM((length, half), f32)] * (2 * last),
        ),
        compiler_params=pltpu.CompilerParams(dimension_semantics=("arbitrary",)),
        name="attend_back",
    )(lo, hi, qkv, qkv, qkv, d_mixed, mixed, lse, seg_row, seg_col, *before)


def bit_of(name):
    axis, step = name
    return (lax.axis_index(axis) // step) % 2


def swap(values, name):
    axis, step = name
    count = lax.axis_size(axis)
    return lax.ppermute(values, axis, [(i, i ^ step) for i in range(count)])


def pick(values, index, dim):
    return lax.dynamic_index_in_dim(values, index, dim, keepdims=False)


def in_order(bit, mine, other, dim=0):
    low = jnp.where(bit == 0, mine, other)
    high = jnp.where(bit == 0, other, mine)
    return jnp.stack([low, high], axis=dim)


def grow(values, names):
    for name in names:
        got = swap(values, name)
        values = in_order(bit_of(name), values, got)
    return values


def sort_blocks(values, names, wanted):
    stacked = list(reversed(names))
    order = [stacked.index(name) for name in wanted]
    count = len(names)
    return values.transpose(order + list(range(count, values.ndim)))


def shrink(values, names, wanted):
    left = list(wanted)
    for name in names:
        dim = left.index(name)
        bit = bit_of(name)
        got = swap(pick(values, 1 - bit, dim), name)
        values = pick(values, bit, dim).astype(f32) + got.astype(f32)
        left.remove(name)
        if left:
            values = values.astype(bf16)
    return values


def norm_stats(values):
    average = jnp.mean(values, axis=-1, keepdims=True)
    centred = values - average
    spread = jnp.mean(centred * centred, axis=-1, keepdims=True)
    inverse = lax.rsqrt(spread + epsilon)
    return centred * inverse, inverse


def norm_back(grad, gain, unit, inverse):
    u = grad * gain
    first = jnp.mean(u, axis=-1, keepdims=True)
    second = jnp.mean(u * unit, axis=-1, keepdims=True)
    return (u - first - unit * second) * inverse


def dot_rows(left, right):
    return lax.dot_general(left, right, (((0,), (0,)), ((), ())), preferred_element_type=f32)


def dot_cols(left, right):
    return lax.dot_general(left, right, (((1,), (1,)), ((), ())), preferred_element_type=f32)


def column_sums(values):
    return jnp.sum(values.astype(f32), axis=0)


def on_device(
    tokens, segments, cotangent, query_weight, query_bias, key_weight, value_weight, value_bias,
    output_weight, output_bias, first_gain, first_shift, inner_weight, inner_bias, outer_weight,
    outer_bias, second_gain, second_shift,
):
    core = ("c", 1)
    partner = ("y", 1)
    y = bit_of(partner)
    c = bit_of(core)
    local, width = tokens.shape[1], tokens.shape[2]
    own, hidden = inner_weight.shape
    half = width // 2
    length = segments.shape[1]
    chunks = hidden // width
    bits = lambda axis: [(axis, 1 << k) for k in reversed(range(lax.axis_size(axis).bit_length() - 1))]
    y_names = bits("y")
    far, near = bits("dp")[:-1], bits("dp")[-1]
    wanted = bits("dp") + y_names
    team = y_names[:-1]
    rank = lax.axis_index("y") // 2
    blocks = (2,) * len(wanted)

    columns = jnp.stack(
        [query_bias, value_bias, output_bias, first_gain, first_shift, outer_bias, second_gain, second_shift],
        axis=1,
    )
    columns = jnp.concatenate([columns, inner_bias.reshape(own, chunks)], axis=1)
    columns = jnp.pad(columns, ((0, 0), (0, PAIR - columns.shape[1])))

    def three(index):
        return jnp.concatenate(
            [lax.dynamic_slice_in_dim(w, index * half, half, 1) for w in (query_weight, key_weight, value_weight)]
            + [columns],
            axis=1,
        )

    attention_part = in_order(c, three(c), swap(three(1 - c), core)).reshape(2 * own, 3 * half + PAIR)

    def to_chip(values):
        return in_order(y, pick(values, y, 0), swap(pick(values, 1 - y, 0), partner))

    mine = to_chip(tokens)
    source_all = grow(in_order(c, mine, swap(mine, core), 1), team).reshape(length, width)
    source = mine.reshape(2 * local, width)

    attention_part = grow(attention_part, far)
    cut = (3 * half + PAIR) // 2 // 128 * 128
    output_inner = jnp.concatenate([output_weight, inner_weight], axis=1)
    output_inner, outer_part, attention_part = lax.optimization_barrier((output_inner, outer_weight, attention_part))
    part_a = grow(attention_part[..., :cut], [near] + y_names)
    part_b = grow(attention_part[..., cut:], y_names + [near])
    part_a = sort_blocks(part_a, far + [near] + y_names, wanted).reshape(width, cut)
    part_b = sort_blocks(part_b, far + y_names + [near], wanted).reshape(width, 3 * half + PAIR - cut)
    joined = jnp.concatenate([part_a, part_b], axis=1)
    qkv_weight = joined[:, : 3 * half]
    vectors = joined[:, 3 * half :].astype(f32).T
    half_of = lambda row: lax.dynamic_slice_in_dim(row, c * half, half, 0)
    qkv_bias = jnp.concatenate([half_of(vectors[0]), jnp.zeros((half,), f32), half_of(vectors[1])])
    output_bias, first_gain, first_shift, outer_bias, second_gain, second_shift = [vectors[k] for k in range(2, 8)]
    inner_bias = joined[:, 3 * half + 8 : 3 * half + 8 + chunks].reshape(hidden).astype(f32)

    output_inner = grow(output_inner, far)
    outer_part = grow(outer_part, far)
    output_inner = sort_blocks(grow(output_inner, [near] + y_names), far + [near] + y_names, wanted)
    outer_part = sort_blocks(grow(outer_part, y_names + [near]), far + y_names + [near], wanted)
    output_inner = in_order(c, output_inner, swap(output_inner, core), len(wanted)).reshape(width, width + hidden)
    outer_weight = in_order(c, outer_part, swap(outer_part, core), len(wanted)).reshape(hidden, width)
    output_weight = output_inner[:, :width]
    inner_weight = output_inner[:, width:]

    seg = pick(segments, y, 0)
    lo, hi = key_range(seg)
    seg_row = jnp.broadcast_to(seg[None, :], (8, length))
    seg_col = jnp.broadcast_to(seg[:, None], (length, PAIR))
    qkv = (dot(source_all, qkv_weight) + qkv_bias).astype(bf16)
    attended = []
    steps = length // BQ
    marks = [0, (3 * steps + 7) // 8, (6 * steps + 7) // 8, steps]
    for p in range(3):
        attended.append(attend(qkv, marks[p], marks[p + 1] - marks[p], seg_row, seg_col, lo, hi))
    mixed_all = jnp.concatenate([a[0] for a in attended], axis=0)
    log_sums = jnp.concatenate([a[1] for a in attended], axis=1)
    mixed_heads = pick(mixed_all.reshape(-1, 2, 2, local, half), rank, 0)
    got = swap(pick(mixed_heads, 1 - c, 1), core)
    mixed = in_order(c, pick(mixed_heads, c, 1), got, 2).reshape(2 * local, width)

    pre = source.astype(f32) + dot(mixed, output_weight) + output_bias
    first_unit, first_inverse = norm_stats(pre)
    first = first_unit * first_gain + first_shift
    first_low = first.astype(bf16)
    inner = dot(first_low, inner_weight) + inner_bias
    phi = 0.5 * (1.0 + lax.erf(inner * math.sqrt(0.5)))
    active = (inner * phi).astype(bf16)
    slope = (phi + inner * (jnp.exp(-0.5 * inner * inner) * (1.0 / math.sqrt(2.0 * math.pi)))).astype(bf16)
    total = first + dot(active, outer_weight) + outer_bias
    second_unit, second_inverse = norm_stats(total)
    result = (second_unit * second_gain + second_shift).astype(bf16).reshape(2, local, width)

    def to_owner(values):
        kept = pick(values, y, 0)
        return in_order(y, kept, swap(pick(values, 1 - y, 0).astype(bf16), partner).astype(kept.dtype))

    layer_output = to_owner(result)

    grad = to_chip(cotangent).reshape(2 * local, width).astype(f32)
    d_total = norm_back(grad, second_gain, second_unit, second_inverse)
    d_second_gain = jnp.sum(grad * second_unit, axis=0)
    d_second_shift = jnp.sum(grad, axis=0)
    d_outer = d_total.astype(bf16)

    def core_then_chips(gradient, names):
        gradient = gradient.astype(bf16)
        rows, cols = gradient.shape
        shaped = gradient.reshape(blocks + (2, rows // (2 * math.prod(blocks)), cols))
        dim = len(wanted)
        got = swap(pick(shaped, 1 - c, dim), core)
        summed = (pick(shaped, c, dim).astype(f32) + got.astype(f32)).astype(bf16)
        return shrink(summed, names, wanted)

    back = list(reversed(far))
    g_outer_weight = core_then_chips(dot_rows(active, d_outer), [near] + y_names + back)
    d_inner = (dot_cols(d_outer, outer_weight) * slope.astype(f32)).astype(bf16)
    g_inner_weight = core_then_chips(dot_rows(first_low, d_inner), y_names + [near] + back)
    d_first = dot_cols(d_inner, inner_weight) + d_total
    d_pre = norm_back(d_first, first_gain, first_unit, first_inverse)
    d_attended = d_pre.astype(bf16)
    d_mixed = dot_cols(d_attended, output_weight).astype(bf16)
    d_mixed = d_mixed.reshape(2 * local, 2, half)
    got = swap(pick(d_mixed, 1 - c, 1), core)
    d_heads = in_order(c, pick(d_mixed, c, 1).reshape(2, local, half), got.reshape(2, local, half), 1)
    d_heads = grow(d_heads, reversed(team)).reshape(length, half)

    g_columns = jnp.stack(
        [
            column_sums(d_attended),
            jnp.sum(d_first * first_unit, axis=0),
            jnp.sum(d_first, axis=0),
            column_sums(d_outer),
            d_second_gain,
            d_second_shift,
        ],
        axis=1,
    )
    g_columns = jnp.concatenate([g_columns, column_sums(d_inner).reshape(width, chunks)], axis=1)
    g_columns = jnp.pad(g_columns, ((0, 0), (0, PAIR - g_columns.shape[1])))
    g_output = core_then_chips(
        jnp.concatenate([dot_rows(mixed, d_attended), g_columns], axis=1), y_names + [near] + back
    )

    part = attend_back(qkv, 0, steps // 2, (), mixed_all, d_heads, log_sums, seg_row, seg_col, lo, hi)
    rest = attend_back(
        qkv, steps // 2, steps - steps // 2, part[1:], mixed_all, d_heads, log_sums, seg_row, seg_col, lo, hi
    )
    d_qkv = jnp.concatenate([jnp.concatenate([part[0], rest[0]], axis=0), rest[1], rest[2]], axis=1)
    place = lambda part: lax.dynamic_update_slice_in_dim(
        jnp.zeros((width,), f32), column_sums(d_qkv[:, part * half : (part + 1) * half]), c * half, 0
    )
    g_bias = jnp.pad(jnp.stack([place(0), place(2)], axis=1), ((0, 0), (0, PAIR - 2)))
    g_qkv = dot_rows(source_all, d_qkv)
    g_qkv = jnp.concatenate([g_qkv, g_bias], axis=1).astype(bf16)
    if team:
        g_qkv = jnp.where(rank == 0, g_qkv, jnp.zeros_like(g_qkv))
    g_qkv = g_qkv.reshape(blocks + (2 * own, 3 * half + PAIR))
    g_a = shrink(g_qkv[..., :cut], y_names + [near] + back, wanted)
    g_b = shrink(g_qkv[..., cut:], [near] + y_names + back, wanted)
    g_chip = jnp.concatenate([g_a, g_b], axis=1).reshape(2, own, 3 * half + PAIR)
    kept = pick(g_chip, c, 0)
    got = swap(pick(g_chip, 1 - c, 0), core)
    g_weights = in_order(c, kept[:, : 3 * half], got[:, : 3 * half])
    g_biases = kept[:, 3 * half :] + got[:, 3 * half :]
    g_three = [
        jnp.concatenate([g_weights[0, :, k * half : (k + 1) * half], g_weights[1, :, k * half : (k + 1) * half]], axis=1)
        for k in range(3)
    ]

    shaped = pick(d_qkv.reshape(-1, 2, 2, local, 3 * half), rank, 0)
    other = dot_cols(pick(shaped, 1 - c, 1).reshape(2 * local, 3 * half), qkv_weight).astype(bf16)
    other = swap(other, core)
    d_input = d_pre + dot_cols(pick(shaped, c, 1).reshape(2 * local, 3 * half), qkv_weight) + other.astype(f32)
    input_gradient = to_owner(d_input.reshape(2, local, width))

    return (
        layer_output,
        input_gradient,
        g_three[0],
        g_biases[:, 0],
        g_three[1],
        g_three[2],
        g_biases[:, 1],
        g_output[:, :width],
        g_output[:, width],
        g_output[:, width + 1],
        g_output[:, width + 2],
        g_inner_weight,
        g_output[:, width + 6 : width + 6 + chunks].reshape(own * chunks),
        g_outer_weight,
        g_output[:, width + 3],
        g_output[:, width + 4],
        g_output[:, width + 5],
    )


def solution(mesh):
    dp, ctx = mesh.shape["dp"], mesh.shape["ctx"]
    split = Mesh(mesh.devices.reshape(dp, ctx // 2, 2), ("dp", "y", "c"))
    every = ("dp", "y", "c")
    tokens = P("dp", ("y", "c"), None)
    matrix = P(every, None)
    vector = P(every)

    return jax.shard_map(
        on_device,
        mesh=split,
        in_specs=(
            tokens, P("dp", None), tokens,
            matrix, vector, matrix, matrix, vector, matrix, vector, vector, vector,
            matrix, vector, matrix, vector, vector, vector,
        ),
        out_specs=(
            tokens, tokens,
            matrix, vector, matrix, matrix, vector, matrix, vector, vector, vector,
            matrix, vector, matrix, vector, vector, vector,
        ),
        check_vma=False,
    )
```

```python
import functools
import math

import jax
import jax.numpy as jnp
from jax import lax
from jax.experimental import pallas as pl
from jax.experimental.pallas import tpu as pltpu
from jax.sharding import Mesh
from jax.sharding import PartitionSpec as P

from jax.sharding import Mesh
from jax.sharding import PartitionSpec as P

HEAD = 64
PAIR = 2 * HEAD
BQ = 256
BK = 256
LOG2E = math.log2(math.e)
epsilon = 1e-05
f32 = jnp.float32
bf16 = jnp.bfloat16


def dot(left, right):
    return jnp.dot(left, right, preferred_element_type=f32)


def lanes_of(shape, head):
    lane = lax.broadcasted_iota(jnp.int32, shape, 1)
    return (lane < HEAD) if head == 0 else (lane >= HEAD)


def rows_of(shape, head):
    row = lax.broadcasted_iota(jnp.int32, shape, 0)
    return (row < HEAD) if head == 0 else (row >= HEAD)


def attend_kernel(lo, hi, q_ref, k_ref, v_ref, seg_col_ref, seg_row_ref, o_ref, lse_ref, kt_ref, v_scr, *, base):
    step = pl.program_id(0)
    group = q_ref.shape[1] // PAIR
    heads = [(p, h) for p in range(group) for h in (0, 1)]
    at_pair = [slice(p * PAIR, (p + 1) * PAIR) for p in range(group)]

    @pl.when(step == 0)
    def _():
        for p in range(group):
            kt_ref[at_pair[p], :] = k_ref[:, at_pair[p]].astype(f32).T.astype(bf16)
            values = v_ref[:, at_pair[p]].astype(f32)
            for h in (0, 1):
                v_scr[2 * p + h] = jnp.where(lanes_of(values.shape, h), values, 1.0).astype(bf16)

    split = []
    for p in range(group):
        queries = q_ref[:, at_pair[p]].astype(f32)
        split += [jnp.where(lanes_of(queries.shape, h), queries, 0.0).astype(bf16) for h in (0, 1)]
    seg_q = seg_col_ref[:, 0:1]

    def one(block, carry):
        at = pl.multiple_of(block * BK, BK)
        allowed = seg_q == seg_row_ref[0:1, pl.ds(at, BK)]
        out = []
        for n, (p, h) in enumerate(heads):
            peak, acc = carry[2 * n], carry[2 * n + 1]
            scores = dot(split[n], kt_ref[at_pair[p], pl.ds(at, BK)])
            scores = jnp.where(allowed, scores * (LOG2E / math.sqrt(HEAD)), -1e30)
            top = jnp.maximum(peak, jnp.max(scores, axis=1, keepdims=True))
            probs = jnp.exp2(scores - top)
            acc = acc * jnp.exp2(peak - top) + dot(probs.astype(bf16), v_scr[n, pl.ds(at, BK), :])
            out += [top, acc]
        return tuple(out)

    start = (jnp.full((BQ, 1), -1e30, f32), jnp.zeros((BQ, PAIR), f32)) * len(heads)
    done = lax.fori_loop(lo[base + step], hi[base + step], one, start)
    for p in range(group):
        peak0, acc0, peak1, acc1 = done[4 * p : 4 * p + 4]
        sums0 = pltpu.roll(acc0, HEAD, 1)
        sums1 = pltpu.roll(acc1, HEAD, 1)
        first = lanes_of(acc0.shape, 0)
        o_ref[:, at_pair[p]] = (jnp.where(first, acc0, acc1) / jnp.where(first, sums0, sums1)).astype(bf16)
        logs = jnp.where(first, peak1 + jnp.log2(acc1), peak0 + jnp.log2(acc0)).T
        lse_ref[16 * p : 16 * p + 8, :] = logs[HEAD : HEAD + 8, :]
        lse_ref[16 * p + 8 : 16 * p + 16, :] = logs[0:8, :]


def attend_back_kernel(
    lo, hi, q_ref, k_ref, v_ref, do_ref, o_ref, lse_ref, seg_row_ref, seg_col_ref, *refs, base, last
):
    if last:
        dk_before, dv_before, dq_ref, dk_ref, dv_ref, kt_ref, dk_acc, dv_acc = refs
    else:
        dq_ref, dk_acc, dv_acc, kt_ref = refs
    step = pl.program_id(0)
    group = q_ref.shape[1] // PAIR
    at_pair = [slice(p * PAIR, (p + 1) * PAIR) for p in range(group)]

    @pl.when(step == 0)
    def _():
        for p in range(group):
            kt_ref[at_pair[p], :] = k_ref[:, at_pair[p]].astype(f32).T.astype(bf16)
        dk_acc[...] = dk_before[...] if last else jnp.zeros_like(dk_acc)
        dv_acc[...] = dv_before[...] if last else jnp.zeros_like(dv_acc)

    q_rows, g_rows, q_cols, g_cols, mean, logs = [], [], [], [], [], []
    for p in range(group):
        queries = q_ref[:, at_pair[p]].astype(f32)
        grads = do_ref[:, at_pair[p]].astype(f32)
        queries_t = queries.T
        grads_t = grads.T
        inner_t = grads_t * o_ref[:, at_pair[p]].astype(f32).T
        for h in (0, 1):
            q_rows.append(jnp.where(lanes_of(queries.shape, h), queries, 0.0).astype(bf16))
            g_rows.append(jnp.where(lanes_of(grads.shape, h), grads, 0.0).astype(bf16))
            q_cols.append(jnp.where(rows_of(queries_t.shape, h), queries_t, 0.0).astype(bf16))
            g_cols.append(jnp.where(rows_of(grads_t.shape, h), grads_t, 0.0).astype(bf16))
            mean.append(jnp.sum(inner_t[h * HEAD : (h + 1) * HEAD, :], axis=0, keepdims=True))
            logs.append(lse_ref[16 * p + 8 * h : 16 * p + 8 * h + 1, :])
    seg_q = seg_row_ref[0:1, :]

    def one(block, carry):
        at = pl.multiple_of(block * BK, BK)
        allowed = seg_col_ref[pl.ds(at, BK), 0:1] == seg_q
        out = []
        for p in range(group):
            keys = k_ref[pl.ds(at, BK), at_pair[p]]
            values = v_ref[pl.ds(at, BK), at_pair[p]]
            probs, scores_grad = [], []
            for h in (0, 1):
                n = 2 * p + h
                scores = dot(keys, q_cols[n]) * (LOG2E / math.sqrt(HEAD)) - logs[n]
                weight = jnp.exp2(jnp.where(allowed, scores, -1e30))
                ds = (weight * (dot(values, g_cols[n]) - mean[n])).astype(bf16)
                probs.append(weight.astype(bf16))
                scores_grad.append(ds)
                rows = slice(p * PAIR + h * HEAD, p * PAIR + (h + 1) * HEAD)
                out.append(carry[n] + dot(kt_ref[rows, pl.ds(at, BK)], ds))
            n = 2 * p
            dv_acc[pl.ds(at, BK), at_pair[p]] += dot(probs[0], g_rows[n]) + dot(probs[1], g_rows[n + 1])
            dk_acc[pl.ds(at, BK), at_pair[p]] += dot(scores_grad[0], q_rows[n]) + dot(scores_grad[1], q_rows[n + 1])
        return tuple(out)

    start = (jnp.zeros((HEAD, BQ), f32),) * (2 * group)
    done = lax.fori_loop(lo[base + step], hi[base + step], one, start)
    for p in range(group):
        turned = jnp.concatenate([done[2 * p], done[2 * p + 1]], axis=0).T
        dq_ref[:, at_pair[p]] = (turned * (1.0 / math.sqrt(HEAD))).astype(bf16)

    if not last:
        return

    @pl.when(step == pl.num_programs(0) - 1)
    def _():
        dk_ref[...] = (dk_acc[...] * (1.0 / math.sqrt(HEAD))).astype(bf16)
        dv_ref[...] = dv_acc[...].astype(bf16)


def key_range(seg):
    blocks = seg.reshape(-1, BQ)
    first = jnp.sum(seg[None, :] < blocks[:, :1], axis=1, dtype=jnp.int32)
    last = jnp.sum(seg[None, :] <= blocks[:, -1:], axis=1, dtype=jnp.int32)
    return first // BK, (last + BK - 1) // BK


def attend(qkv, base, count, seg_row, seg_col, lo, hi):
    length, wide = qkv.shape
    half = wide // 3
    whole = lambda part: pl.BlockSpec((length, half), lambda i, lo, hi: (0, part))
    return pl.pallas_call(
        functools.partial(attend_kernel, base=base),
        out_shape=(
            jax.ShapeDtypeStruct((count * BQ, half), bf16),
            jax.ShapeDtypeStruct((half // PAIR * 16, count * BQ), f32),
        ),
        grid_spec=pltpu.PrefetchScalarGridSpec(
            num_scalar_prefetch=2,
            grid=(count,),
            in_specs=[
                pl.BlockSpec((BQ, half), lambda i, lo, hi: (base + i, 0)),
                whole(1),
                whole(2),
                pl.BlockSpec((BQ, PAIR), lambda i, lo, hi: (base + i, 0)),
                pl.BlockSpec((8, length), lambda i, lo, hi: (0, 0)),
            ],
            out_specs=[
                pl.BlockSpec((BQ, half), lambda i, lo, hi: (i, 0)),
                pl.BlockSpec((half // PAIR * 16, BQ), lambda i, lo, hi: (0, i)),
            ],
            scratch_shapes=[
                pltpu.VMEM((half, length), bf16),
                pltpu.VMEM((half // HEAD, length, PAIR), bf16),
            ],
        ),
        compiler_params=pltpu.CompilerParams(dimension_semantics=("arbitrary",)),
        name="attend",
    )(lo, hi, qkv, qkv, qkv, seg_col, seg_row)


def attend_back(qkv, base, count, before, mixed, d_mixed, lse, seg_row, seg_col, lo, hi):
    length, wide = qkv.shape
    half = wide // 3
    whole = lambda part: pl.BlockSpec((length, half), lambda i, lo, hi: (0, part))
    rows = pl.BlockSpec((BQ, half), lambda i, lo, hi: (base + i, 0))
    last = bool(before)
    kind = bf16 if last else f32
    return pl.pallas_call(
        functools.partial(attend_back_kernel, base=base, last=last),
        out_shape=(
            jax.ShapeDtypeStruct((count * BQ, half), bf16),
            jax.ShapeDtypeStruct((length, half), kind),
            jax.ShapeDtypeStruct((length, half), kind),
        ),
        grid_spec=pltpu.PrefetchScalarGridSpec(
            num_scalar_prefetch=2,
            grid=(count,),
            in_specs=[
                rows,
                whole(1),
                whole(2),
                rows,
                rows,
                pl.BlockSpec((half // PAIR * 16, BQ), lambda i, lo, hi: (0, base + i)),
                pl.BlockSpec((8, BQ), lambda i, lo, hi: (0, base + i)),
                pl.BlockSpec((length, PAIR), lambda i, lo, hi: (0, 0)),
            ]
            + [whole(0)] * len(before),
            out_specs=[pl.BlockSpec((BQ, half), lambda i, lo, hi: (i, 0)), whole(0), whole(0)],
            scratch_shapes=[pltpu.VMEM((half, length), bf16)] + [pltpu.VMEM((length, half), f32)] * (2 * last),
        ),
        compiler_params=pltpu.CompilerParams(dimension_semantics=("arbitrary",)),
        name="attend_back",
    )(lo, hi, qkv, qkv, qkv, d_mixed, mixed, lse, seg_row, seg_col, *before)


def bit_of(name):
    axis, step = name
    return (lax.axis_index(axis) // step) % 2


def swap(values, name):
    axis, step = name
    count = lax.axis_size(axis)
    return lax.ppermute(values, axis, [(i, i ^ step) for i in range(count)])


def pick(values, index, dim):
    return lax.dynamic_index_in_dim(values, index, dim, keepdims=False)


def in_order(bit, mine, other, dim=0):
    mine, other = jnp.expand_dims(mine, dim), jnp.expand_dims(other, dim)
    place = lax.broadcasted_iota(jnp.int32, (1,) * dim + (2,) + (1,) * (mine.ndim - dim - 1), dim)
    return jnp.where(place == bit, mine, other)


def grow(values, names):
    for name in names:
        got = swap(values, name)
        values = in_order(bit_of(name), values, got)
    return values


def sort_blocks(values, names, wanted):
    stacked = list(reversed(names))
    order = [stacked.index(name) for name in wanted]
    count = len(names)
    return values.transpose(order + list(range(count, values.ndim)))


def shrink(values, names, wanted):
    left = list(wanted)
    for name in names:
        dim = left.index(name)
        bit = bit_of(name)
        got = swap(pick(values, 1 - bit, dim), name)
        left.remove(name)
        values = pick(values, bit, dim).astype(f32) + got.astype(f32)
        if left:
            values = values.astype(bf16)
    return values


def norm_stats(values):
    average = jnp.mean(values, axis=-1, keepdims=True)
    centred = values - average
    spread = jnp.mean(centred * centred, axis=-1, keepdims=True)
    inverse = lax.rsqrt(spread + epsilon)
    return centred * inverse, inverse


def norm_back(grad, gain, unit, inverse):
    u = grad * gain
    first = jnp.mean(u, axis=-1, keepdims=True)
    second = jnp.mean(u * unit, axis=-1, keepdims=True)
    return (u - first - unit * second) * inverse


def dot_rows(left, right):
    return lax.dot_general(left, right, (((0,), (0,)), ((), ())), preferred_element_type=f32)


def dot_cols(left, right):
    return lax.dot_general(left, right, (((1,), (1,)), ((), ())), preferred_element_type=f32)


def column_sums(values):
    return jnp.sum(values.astype(f32), axis=0)


def on_device(
    tokens, segments, cotangent, query_weight, query_bias, key_weight, value_weight, value_bias,
    output_weight, output_bias, first_gain, first_shift, inner_weight, inner_bias, outer_weight,
    outer_bias, second_gain, second_shift,
):
    core = ("c", 1)
    partner = ("y", 1)
    y = bit_of(partner)
    c = bit_of(core)
    local, width = tokens.shape[1], tokens.shape[2]
    own, hidden = inner_weight.shape
    half = width // 2
    length = segments.shape[1]
    chunks = hidden // width
    bits = lambda axis: [(axis, 1 << k) for k in reversed(range(lax.axis_size(axis).bit_length() - 1))]
    y_names = bits("y")
    far, near = bits("dp")[:-1], bits("dp")[-1]
    wanted = bits("dp") + y_names
    team = y_names[:-1]
    rank = lax.axis_index("y") // 2
    blocks = (2,) * len(wanted)

    columns = jnp.concatenate(
        [
            query_bias, value_bias, output_bias, first_gain, first_shift, outer_bias, second_gain, second_shift,
            inner_bias,
        ]
    )
    used = columns.shape[0]
    lines = -(-used // PAIR)
    columns = jnp.pad(columns, (0, lines * PAIR - used)).reshape(lines, PAIR)
    columns = jnp.pad(columns, ((0, own - lines), (0, 0)))

    def three(index):
        return jnp.concatenate(
            [lax.dynamic_slice_in_dim(w, index * half, half, 1) for w in (query_weight, key_weight, value_weight)]
            + [columns],
            axis=1,
        )

    attention_part = in_order(c, three(c), swap(three(1 - c), core)).reshape(2 * own, 3 * half + PAIR)

    def to_chip(values):
        return in_order(y, pick(values, y, 0), swap(pick(values, 1 - y, 0), partner))

    mine = to_chip(tokens)
    source_all = grow(in_order(c, mine, swap(mine, core), 1), team).reshape(length, width)
    source = mine.reshape(2 * local, width)

    attention_part = grow(attention_part, far)
    cut = (3 * half + PAIR) // 2 // 128 * 128
    output_inner = jnp.concatenate([output_weight, inner_weight], axis=1)
    output_inner, outer_part, attention_part = lax.optimization_barrier((output_inner, outer_weight, attention_part))
    part_a = grow(attention_part[..., :cut], [near] + y_names)
    part_b = grow(attention_part[..., cut:], y_names + [near])
    part_a = sort_blocks(part_a, far + [near] + y_names, wanted).reshape(width, cut)
    part_b = sort_blocks(part_b, far + y_names + [near], wanted).reshape(width, 3 * half + PAIR - cut)
    joined = jnp.concatenate([part_a, part_b], axis=1)
    qkv_weight = joined[:, : 3 * half]
    vectors = joined[:, 3 * half :].reshape(-1, own, PAIR)[:, :lines].reshape(-1, lines * PAIR).astype(f32)
    inner_bias = vectors[:, 8 * own : used].reshape(hidden)
    vectors = vectors[:, : 8 * own].reshape(-1, 8, own).transpose(1, 0, 2).reshape(8, width)
    half_of = lambda row: lax.dynamic_slice_in_dim(row, c * half, half, 0)
    qkv_bias = jnp.concatenate([half_of(vectors[0]), jnp.zeros((half,), f32), half_of(vectors[1])])
    output_bias, first_gain, first_shift, outer_bias, second_gain, second_shift = [vectors[k] for k in range(2, 8)]

    output_inner = grow(output_inner, far)
    outer_part = grow(outer_part, far)
    output_inner = sort_blocks(grow(output_inner, [near] + y_names), far + [near] + y_names, wanted)
    outer_part = sort_blocks(grow(outer_part, y_names + [near]), far + y_names + [near], wanted)
    output_inner = in_order(c, output_inner, swap(output_inner, core), len(wanted)).reshape(width, width + hidden)
    outer_weight = in_order(c, outer_part, swap(outer_part, core), len(wanted)).reshape(hidden, width)
    output_weight = output_inner[:, :width]
    inner_weight = output_inner[:, width:]

    seg = pick(segments, y, 0)
    lo, hi = key_range(seg)
    seg_row = jnp.broadcast_to(seg[None, :], (8, length))
    seg_col = jnp.broadcast_to(seg[:, None], (length, PAIR))
    qkv = (dot(source_all, qkv_weight) + qkv_bias).astype(bf16)
    attended = []
    steps = length // BQ
    marks = [0, (3 * steps + 7) // 8, (6 * steps + 7) // 8, steps]
    for p in range(3):
        attended.append(attend(qkv, marks[p], marks[p + 1] - marks[p], seg_row, seg_col, lo, hi))
    mixed_all = jnp.concatenate([a[0] for a in attended], axis=0)
    log_sums = jnp.concatenate([a[1] for a in attended], axis=1)
    mixed_heads = pick(mixed_all.reshape(-1, 2, 2, local, half), rank, 0)
    got = swap(pick(mixed_heads, 1 - c, 1), core).reshape(2 * local, half)
    kept = pick(mixed_heads, c, 1).reshape(2 * local, half)
    weight_kept = lax.dynamic_slice_in_dim(output_weight, c * half, half, 0)
    weight_got = lax.dynamic_slice_in_dim(output_weight, (1 - c) * half, half, 0)

    pre = source.astype(f32) + dot(kept, weight_kept) + dot(got, weight_got) + output_bias
    first_unit, first_inverse = norm_stats(pre)
    first = first_unit * first_gain + first_shift
    first_low = first.astype(bf16)
    inner = dot(first_low, inner_weight) + inner_bias
    phi = 0.5 * (1.0 + lax.erf(inner * math.sqrt(0.5)))
    active = (inner * phi).astype(bf16)
    slope = (phi + inner * (jnp.exp(-0.5 * inner * inner) * (1.0 / math.sqrt(2.0 * math.pi)))).astype(bf16)
    total = first + dot(active, outer_weight) + outer_bias
    second_unit, second_inverse = norm_stats(total)
    result = (second_unit * second_gain + second_shift).astype(bf16).reshape(2, local, width)

    def to_owner(values):
        stays = pick(values, y, 0)
        return in_order(y, stays, swap(pick(values, 1 - y, 0).astype(bf16), partner).astype(stays.dtype))

    layer_output = to_owner(result)

    grad = to_chip(cotangent).reshape(2 * local, width).astype(f32)
    d_total = norm_back(grad, second_gain, second_unit, second_inverse)
    d_second_gain = jnp.sum(grad * second_unit, axis=0)
    d_second_shift = jnp.sum(grad, axis=0)
    d_outer = d_total.astype(bf16)

    def core_then_chips(gradient, names):
        gradient = gradient.astype(bf16)
        rows, cols = gradient.shape
        shaped = gradient.reshape(blocks + (2, rows // (2 * math.prod(blocks)), cols))
        dim = len(wanted)
        got = swap(pick(shaped, 1 - c, dim), core)
        summed = (pick(shaped, c, dim).astype(f32) + got.astype(f32)).astype(bf16)
        return shrink(summed, names, wanted)

    back = list(reversed(far))
    g_outer_weight = core_then_chips(dot_rows(active, d_outer), [near] + y_names + back)
    d_inner = (dot_cols(d_outer, outer_weight) * slope.astype(f32)).astype(bf16)
    g_inner = dot_rows(first_low, d_inner)
    g_inner_weight = core_then_chips(g_inner, y_names + [near] + back)
    d_first = dot_cols(d_inner, inner_weight) + d_total
    d_pre = norm_back(d_first, first_gain, first_unit, first_inverse)
    d_attended = d_pre.astype(bf16)
    back_got = dot_cols(d_attended, weight_got).astype(bf16).reshape(2, local, half)
    back_got = swap(back_got, core)
    back_kept = dot_cols(d_attended, weight_kept).astype(bf16).reshape(2, local, half)
    d_heads = in_order(c, back_kept, back_got, 1)
    d_heads = grow(d_heads, reversed(team)).reshape(length, half)

    g_columns = jnp.stack(
        [
            column_sums(d_attended),
            jnp.sum(d_first * first_unit, axis=0),
            jnp.sum(d_first, axis=0),
            column_sums(d_outer),
            d_second_gain,
            d_second_shift,
        ],
        axis=1,
    )
    g_columns = jnp.concatenate([g_columns, column_sums(d_inner).reshape(width, chunks)], axis=1)
    g_columns = jnp.pad(g_columns, ((0, 0), (0, PAIR - g_columns.shape[1])))
    g_output = in_order(c, dot_rows(kept, d_attended).astype(bf16), dot_rows(got, d_attended).astype(bf16))
    g_output = g_output.reshape(width, width)
    g_columns = g_columns.astype(bf16)
    g_output = core_then_chips(jnp.concatenate([g_output, g_columns], axis=1), y_names + [near] + back)

    part = attend_back(qkv, 0, steps // 2, (), mixed_all, d_heads, log_sums, seg_row, seg_col, lo, hi)
    rest = attend_back(
        qkv, steps // 2, steps - steps // 2, part[1:], mixed_all, d_heads, log_sums, seg_row, seg_col, lo, hi
    )
    d_qkv = jnp.concatenate([jnp.concatenate([part[0], rest[0]], axis=0), rest[1], rest[2]], axis=1)
    place = lambda part: lax.dynamic_update_slice_in_dim(
        jnp.zeros((width,), f32), column_sums(d_qkv[:, part * half : (part + 1) * half]), c * half, 0
    )
    g_bias = jnp.pad(jnp.stack([place(0), place(2)], axis=1), ((0, 0), (0, PAIR - 2)))
    g_qkv = dot_rows(source_all, d_qkv)
    g_qkv = jnp.concatenate([g_qkv, g_bias], axis=1).astype(bf16)
    if team:
        g_qkv = jnp.where(rank == 0, g_qkv, jnp.zeros_like(g_qkv))
    g_qkv = g_qkv.reshape(blocks + (2 * own, 3 * half + PAIR))
    g_a = shrink(g_qkv[..., :cut], y_names + [near] + back, wanted)
    g_b = shrink(g_qkv[..., cut:], [near] + y_names + back, wanted)
    g_chip = jnp.concatenate([g_a, g_b], axis=1).reshape(2, own, 3 * half + PAIR)
    chip_kept = pick(g_chip, c, 0)
    chip_got = swap(pick(g_chip, 1 - c, 0), core)
    g_weights = in_order(c, chip_kept[:, : 3 * half], chip_got[:, : 3 * half])
    g_biases = chip_kept[:, 3 * half :] + chip_got[:, 3 * half :]
    g_three = [
        jnp.concatenate([g_weights[0, :, k * half : (k + 1) * half], g_weights[1, :, k * half : (k + 1) * half]], axis=1)
        for k in range(3)
    ]

    shaped = pick(d_qkv.reshape(-1, 2, 2, local, 3 * half), rank, 0)
    other = dot_cols(pick(shaped, 1 - c, 1).reshape(2 * local, 3 * half), qkv_weight).astype(bf16)
    other = swap(other, core)
    d_input = d_pre + dot_cols(pick(shaped, c, 1).reshape(2 * local, 3 * half), qkv_weight) + other.astype(f32)
    input_gradient = to_owner(d_input.reshape(2, local, width))

    return (
        layer_output,
        input_gradient,
        g_three[0],
        g_biases[:, 0],
        g_three[1],
        g_three[2],
        g_biases[:, 1],
        g_output[:, :width],
        g_output[:, width],
        g_output[:, width + 1],
        g_output[:, width + 2],
        g_inner_weight,
        g_output[:, width + 6 : width + 6 + chunks].reshape(own * chunks),
        g_outer_weight,
        g_output[:, width + 3],
        g_output[:, width + 4],
        g_output[:, width + 5],
    )


def solution(mesh):
    dp, ctx = mesh.shape["dp"], mesh.shape["ctx"]
    split = Mesh(mesh.devices.reshape(dp, ctx // 2, 2), ("dp", "y", "c"))
    every = ("dp", "y", "c")
    tokens = P("dp", ("y", "c"), None)
    matrix = P(every, None)
    vector = P(every)

    return jax.shard_map(
        on_device,
        mesh=split,
        in_specs=(
            tokens, P("dp", None), tokens,
            matrix, vector, matrix, matrix, vector, matrix, vector, vector, vector,
            matrix, vector, matrix, vector, vector, vector,
        ),
        out_specs=(
            tokens, tokens,
            matrix, vector, matrix, matrix, vector, matrix, vector, vector, vector,
            matrix, vector, matrix, vector, vector, vector,
        ),
        check_vma=False,
    )
```

```python
import functools
import math

import jax
import jax.numpy as jnp
from jax import lax
from jax.experimental import pallas as pl
from jax.experimental.pallas import tpu as pltpu
from jax.sharding import Mesh
from jax.sharding import PartitionSpec as P

from jax.sharding import Mesh
from jax.sharding import PartitionSpec as P

HEAD = 64
PAIR = 2 * HEAD
BQ = 256
BK = 256
LOG2E = math.log2(math.e)
epsilon = 1e-05
f32 = jnp.float32
bf16 = jnp.bfloat16


def dot(left, right):
    return jnp.dot(left, right, preferred_element_type=f32)


def lanes_of(shape, head):
    lane = lax.broadcasted_iota(jnp.int32, shape, 1)
    return (lane < HEAD) if head == 0 else (lane >= HEAD)


def rows_of(shape, head):
    row = lax.broadcasted_iota(jnp.int32, shape, 0)
    return (row < HEAD) if head == 0 else (row >= HEAD)


def attend_kernel(lo, hi, q_ref, k_ref, v_ref, seg_col_ref, seg_row_ref, o_ref, lse_ref, kt_ref, v_scr, *, base):
    step = pl.program_id(0)
    group = q_ref.shape[1] // PAIR
    heads = [(p, h) for p in range(group) for h in (0, 1)]
    at_pair = [slice(p * PAIR, (p + 1) * PAIR) for p in range(group)]

    @pl.when(step == 0)
    def _():
        for p in range(group):
            kt_ref[at_pair[p], :] = k_ref[:, at_pair[p]].astype(f32).T.astype(bf16)
            values = v_ref[:, at_pair[p]].astype(f32)
            for h in (0, 1):
                v_scr[2 * p + h] = jnp.where(lanes_of(values.shape, h), values, 1.0).astype(bf16)

    split = []
    for p in range(group):
        queries = q_ref[:, at_pair[p]].astype(f32)
        split += [jnp.where(lanes_of(queries.shape, h), queries, 0.0).astype(bf16) for h in (0, 1)]
    seg_q = seg_col_ref[:, 0:1]

    def one(block, carry):
        at = pl.multiple_of(block * BK, BK)
        allowed = seg_q == seg_row_ref[0:1, pl.ds(at, BK)]
        out = []
        for n, (p, h) in enumerate(heads):
            peak, acc = carry[2 * n], carry[2 * n + 1]
            scores = dot(split[n], kt_ref[at_pair[p], pl.ds(at, BK)])
            scores = jnp.where(allowed, scores * (LOG2E / math.sqrt(HEAD)), -1e30)
            top = jnp.maximum(peak, jnp.max(scores, axis=1, keepdims=True))
            probs = jnp.exp2(scores - top)
            acc = acc * jnp.exp2(peak - top) + dot(probs.astype(bf16), v_scr[n, pl.ds(at, BK), :])
            out += [top, acc]
        return tuple(out)

    start = (jnp.full((BQ, 1), -1e30, f32), jnp.zeros((BQ, PAIR), f32)) * len(heads)
    done = lax.fori_loop(lo[base + step], hi[base + step], one, start)
    for p in range(group):
        peak0, acc0, peak1, acc1 = done[4 * p : 4 * p + 4]
        sums0 = pltpu.roll(acc0, HEAD, 1)
        sums1 = pltpu.roll(acc1, HEAD, 1)
        first = lanes_of(acc0.shape, 0)
        o_ref[:, at_pair[p]] = (jnp.where(first, acc0, acc1) / jnp.where(first, sums0, sums1)).astype(bf16)
        logs = jnp.where(first, peak1 + jnp.log2(acc1), peak0 + jnp.log2(acc0)).T
        lse_ref[16 * p : 16 * p + 8, :] = logs[HEAD : HEAD + 8, :]
        lse_ref[16 * p + 8 : 16 * p + 16, :] = logs[0:8, :]


def attend_back_kernel(
    lo, hi, q_ref, k_ref, v_ref, do_ref, o_ref, lse_ref, seg_row_ref, seg_col_ref, *refs, base, last
):
    if last:
        dk_before, dv_before, dq_ref, dk_ref, dv_ref, kt_ref, dk_acc, dv_acc = refs
    else:
        dq_ref, dk_acc, dv_acc, kt_ref = refs
    step = pl.program_id(0)
    group = q_ref.shape[1] // PAIR
    at_pair = [slice(p * PAIR, (p + 1) * PAIR) for p in range(group)]

    @pl.when(step == 0)
    def _():
        for p in range(group):
            kt_ref[at_pair[p], :] = k_ref[:, at_pair[p]].astype(f32).T.astype(bf16)
        dk_acc[...] = dk_before[...] if last else jnp.zeros_like(dk_acc)
        dv_acc[...] = dv_before[...] if last else jnp.zeros_like(dv_acc)

    q_rows, g_rows, q_cols, g_cols, mean, logs = [], [], [], [], [], []
    for p in range(group):
        queries = q_ref[:, at_pair[p]].astype(f32)
        grads = do_ref[:, at_pair[p]].astype(f32)
        queries_t = queries.T
        grads_t = grads.T
        inner_t = grads_t * o_ref[:, at_pair[p]].astype(f32).T
        for h in (0, 1):
            q_rows.append(jnp.where(lanes_of(queries.shape, h), queries, 0.0).astype(bf16))
            g_rows.append(jnp.where(lanes_of(grads.shape, h), grads, 0.0).astype(bf16))
            q_cols.append(jnp.where(rows_of(queries_t.shape, h), queries_t, 0.0).astype(bf16))
            g_cols.append(jnp.where(rows_of(grads_t.shape, h), grads_t, 0.0).astype(bf16))
            mean.append(jnp.sum(inner_t[h * HEAD : (h + 1) * HEAD, :], axis=0, keepdims=True))
            logs.append(lse_ref[16 * p + 8 * h : 16 * p + 8 * h + 1, :])
    seg_q = seg_row_ref[0:1, :]

    def one(block, carry):
        at = pl.multiple_of(block * BK, BK)
        allowed = seg_col_ref[pl.ds(at, BK), 0:1] == seg_q
        out = []
        for p in range(group):
            keys = k_ref[pl.ds(at, BK), at_pair[p]]
            values = v_ref[pl.ds(at, BK), at_pair[p]]
            probs, scores_grad = [], []
            for h in (0, 1):
                n = 2 * p + h
                scores = dot(keys, q_cols[n]) * (LOG2E / math.sqrt(HEAD)) - logs[n]
                weight = jnp.exp2(jnp.where(allowed, scores, -1e30))
                ds = (weight * (dot(values, g_cols[n]) - mean[n])).astype(bf16)
                probs.append(weight.astype(bf16))
                scores_grad.append(ds)
                rows = slice(p * PAIR + h * HEAD, p * PAIR + (h + 1) * HEAD)
                out.append(carry[n] + dot(kt_ref[rows, pl.ds(at, BK)], ds))
            n = 2 * p
            dv_acc[pl.ds(at, BK), at_pair[p]] += dot(probs[0], g_rows[n]) + dot(probs[1], g_rows[n + 1])
            dk_acc[pl.ds(at, BK), at_pair[p]] += dot(scores_grad[0], q_rows[n]) + dot(scores_grad[1], q_rows[n + 1])
        return tuple(out)

    start = (jnp.zeros((HEAD, BQ), f32),) * (2 * group)
    done = lax.fori_loop(lo[base + step], hi[base + step], one, start)
    for p in range(group):
        turned = jnp.concatenate([done[2 * p], done[2 * p + 1]], axis=0).T
        dq_ref[:, at_pair[p]] = (turned * (1.0 / math.sqrt(HEAD))).astype(bf16)

    if not last:
        return

    @pl.when(step == pl.num_programs(0) - 1)
    def _():
        dk_ref[...] = (dk_acc[...] * (1.0 / math.sqrt(HEAD))).astype(bf16)
        dv_ref[...] = dv_acc[...].astype(bf16)


def key_range(seg):
    blocks = seg.reshape(-1, BQ)
    first = jnp.sum(seg[None, :] < blocks[:, :1], axis=1, dtype=jnp.int32)
    last = jnp.sum(seg[None, :] <= blocks[:, -1:], axis=1, dtype=jnp.int32)
    return first // BK, (last + BK - 1) // BK


def attend(qkv, base, count, seg_row, seg_col, lo, hi):
    length, wide = qkv.shape
    half = wide // 3
    whole = lambda part: pl.BlockSpec((length, half), lambda i, lo, hi: (0, part))
    return pl.pallas_call(
        functools.partial(attend_kernel, base=base),
        out_shape=(
            jax.ShapeDtypeStruct((count * BQ, half), bf16),
            jax.ShapeDtypeStruct((half // PAIR * 16, count * BQ), f32),
        ),
        grid_spec=pltpu.PrefetchScalarGridSpec(
            num_scalar_prefetch=2,
            grid=(count,),
            in_specs=[
                pl.BlockSpec((BQ, half), lambda i, lo, hi: (base + i, 0)),
                whole(1),
                whole(2),
                pl.BlockSpec((BQ, PAIR), lambda i, lo, hi: (base + i, 0)),
                pl.BlockSpec((8, length), lambda i, lo, hi: (0, 0)),
            ],
            out_specs=[
                pl.BlockSpec((BQ, half), lambda i, lo, hi: (i, 0)),
                pl.BlockSpec((half // PAIR * 16, BQ), lambda i, lo, hi: (0, i)),
            ],
            scratch_shapes=[
                pltpu.VMEM((half, length), bf16),
                pltpu.VMEM((half // HEAD, length, PAIR), bf16),
            ],
        ),
        compiler_params=pltpu.CompilerParams(dimension_semantics=("arbitrary",)),
        name="attend",
    )(lo, hi, qkv, qkv, qkv, seg_col, seg_row)


def attend_back(qkv, base, count, before, mixed, d_mixed, lse, seg_row, seg_col, lo, hi):
    length, wide = qkv.shape
    half = wide // 3
    whole = lambda part: pl.BlockSpec((length, half), lambda i, lo, hi: (0, part))
    rows = pl.BlockSpec((BQ, half), lambda i, lo, hi: (base + i, 0))
    last = bool(before)
    kind = bf16 if last else f32
    return pl.pallas_call(
        functools.partial(attend_back_kernel, base=base, last=last),
        out_shape=(
            jax.ShapeDtypeStruct((count * BQ, half), bf16),
            jax.ShapeDtypeStruct((length, half), kind),
            jax.ShapeDtypeStruct((length, half), kind),
        ),
        grid_spec=pltpu.PrefetchScalarGridSpec(
            num_scalar_prefetch=2,
            grid=(count,),
            in_specs=[
                rows,
                whole(1),
                whole(2),
                rows,
                rows,
                pl.BlockSpec((half // PAIR * 16, BQ), lambda i, lo, hi: (0, base + i)),
                pl.BlockSpec((8, BQ), lambda i, lo, hi: (0, base + i)),
                pl.BlockSpec((length, PAIR), lambda i, lo, hi: (0, 0)),
            ]
            + [whole(0)] * len(before),
            out_specs=[pl.BlockSpec((BQ, half), lambda i, lo, hi: (i, 0)), whole(0), whole(0)],
            scratch_shapes=[pltpu.VMEM((half, length), bf16)] + [pltpu.VMEM((length, half), f32)] * (2 * last),
        ),
        compiler_params=pltpu.CompilerParams(dimension_semantics=("arbitrary",)),
        name="attend_back",
    )(lo, hi, qkv, qkv, qkv, d_mixed, mixed, lse, seg_row, seg_col, *before)


def bit_of(name):
    axis, step = name
    return (lax.axis_index(axis) // step) % 2


def swap(values, name):
    axis, step = name
    count = lax.axis_size(axis)
    return lax.ppermute(values, axis, [(i, i ^ step) for i in range(count)])


def pick(values, index, dim):
    return lax.dynamic_index_in_dim(values, index, dim, keepdims=False)


def in_order(bit, mine, other, dim=0):
    low = jnp.where(bit == 0, mine, other)
    high = jnp.where(bit == 0, other, mine)
    return jnp.stack([low, high], axis=dim)


def grow(values, names):
    for name in names:
        got = swap(values, name)
        values = in_order(bit_of(name), values, got)
    return values


def sort_blocks(values, names, wanted):
    stacked = list(reversed(names))
    order = [stacked.index(name) for name in wanted]
    count = len(names)
    return values.transpose(order + list(range(count, values.ndim)))


def shrink(values, names, wanted):
    left = list(wanted)
    for name in names:
        dim = left.index(name)
        bit = bit_of(name)
        got = swap(pick(values, 1 - bit, dim), name)
        left.remove(name)
        values = pick(values, bit, dim).astype(f32) + got.astype(f32)
        if left:
            values = values.astype(bf16)
    return values


def norm_stats(values):
    average = jnp.mean(values, axis=-1, keepdims=True)
    centred = values - average
    spread = jnp.mean(centred * centred, axis=-1, keepdims=True)
    inverse = lax.rsqrt(spread + epsilon)
    return centred * inverse, inverse


def norm_back(grad, gain, unit, inverse):
    u = grad * gain
    first = jnp.mean(u, axis=-1, keepdims=True)
    second = jnp.mean(u * unit, axis=-1, keepdims=True)
    return (u - first - unit * second) * inverse


def dot_rows(left, right):
    return lax.dot_general(left, right, (((0,), (0,)), ((), ())), preferred_element_type=f32)


def dot_cols(left, right):
    return lax.dot_general(left, right, (((1,), (1,)), ((), ())), preferred_element_type=f32)


def column_sums(values):
    return jnp.sum(values.astype(f32), axis=0)


def on_device(
    tokens, segments, cotangent, query_weight, query_bias, key_weight, value_weight, value_bias,
    output_weight, output_bias, first_gain, first_shift, inner_weight, inner_bias, outer_weight,
    outer_bias, second_gain, second_shift,
):
    core = ("c", 1)
    partner = ("y", 1)
    y = bit_of(partner)
    c = bit_of(core)
    local, width = tokens.shape[1], tokens.shape[2]
    own, hidden = inner_weight.shape
    half = width // 2
    length = segments.shape[1]
    chunks = hidden // width
    bits = lambda axis: [(axis, 1 << k) for k in reversed(range(lax.axis_size(axis).bit_length() - 1))]
    y_names = bits("y")
    far, near = bits("dp")[:-1], bits("dp")[-1]
    wanted = bits("dp") + y_names
    team = y_names[:-1]
    rank = lax.axis_index("y") // 2
    blocks = (2,) * len(wanted)

    def in_rows(*vectors):
        flat = jnp.concatenate(vectors)
        lines = -(-flat.shape[0] // PAIR)
        flat = jnp.pad(flat, (0, lines * PAIR - flat.shape[0])).reshape(lines, PAIR)
        return jnp.pad(flat, ((0, own - lines), (0, 0)))

    def from_rows(block, count):
        lines = -(-count * own // PAIR)
        flat = block.reshape(-1, own, PAIR)[:, :lines].reshape(-1, lines * PAIR).astype(f32)
        return flat[:, : count * own]

    columns = in_rows(query_bias, value_bias)
    others = in_rows(output_bias, first_gain, first_shift, outer_bias, second_gain, second_shift, inner_bias)

    def three(index):
        return jnp.concatenate(
            [lax.dynamic_slice_in_dim(w, index * half, half, 1) for w in (query_weight, key_weight, value_weight)]
            + [columns],
            axis=1,
        )

    attention_part = in_order(c, three(c), swap(three(1 - c), core)).reshape(2 * own, 3 * half + PAIR)

    def to_chip(values):
        return in_order(y, pick(values, y, 0), swap(pick(values, 1 - y, 0), partner))

    mine = to_chip(tokens)
    source_all = grow(in_order(c, mine, swap(mine, core), 1), team).reshape(length, width)
    source = mine.reshape(2 * local, width)

    attention_part = grow(attention_part, far)
    cut = (3 * half + PAIR) // 2 // 128 * 128
    output_inner = jnp.concatenate([output_weight, inner_weight, others], axis=1)
    output_inner, outer_part, attention_part = lax.optimization_barrier((output_inner, outer_weight, attention_part))
    part_a = grow(attention_part[..., :cut], [near] + y_names)
    part_b = grow(attention_part[..., cut:], y_names + [near])
    part_a = sort_blocks(part_a, far + [near] + y_names, wanted).reshape(width, cut)
    part_b = sort_blocks(part_b, far + y_names + [near], wanted).reshape(width, 3 * half + PAIR - cut)
    joined = jnp.concatenate([part_a, part_b], axis=1)
    qkv_weight = joined[:, : 3 * half]
    vectors = from_rows(joined[:, 3 * half :], 2).reshape(-1, 2, own).transpose(1, 0, 2).reshape(2, width)
    half_of = lambda row: lax.dynamic_slice_in_dim(row, c * half, half, 0)
    qkv_bias = jnp.concatenate([half_of(vectors[0]), jnp.zeros((half,), f32), half_of(vectors[1])])

    output_inner = grow(output_inner, far)
    outer_part = grow(outer_part, far)
    output_inner = sort_blocks(grow(output_inner, [near] + y_names), far + [near] + y_names, wanted)
    outer_part = sort_blocks(grow(outer_part, y_names + [near]), far + y_names + [near], wanted)
    output_inner = in_order(c, output_inner, swap(output_inner, core), len(wanted)).reshape(width, width + hidden + PAIR)
    outer_weight = in_order(c, outer_part, swap(outer_part, core), len(wanted)).reshape(hidden, width)
    output_weight = output_inner[:, :width]
    inner_weight = output_inner[:, width : width + hidden]
    vectors = from_rows(output_inner[:, width + hidden :], 6 + chunks)
    inner_bias = vectors[:, 6 * own :].reshape(hidden)
    vectors = vectors[:, : 6 * own].reshape(-1, 6, own).transpose(1, 0, 2).reshape(6, width)
    output_bias, first_gain, first_shift, outer_bias, second_gain, second_shift = [vectors[k] for k in range(6)]

    seg = pick(segments, y, 0)
    lo, hi = key_range(seg)
    seg_row = jnp.broadcast_to(seg[None, :], (8, length))
    seg_col = jnp.broadcast_to(seg[:, None], (length, PAIR))
    qkv = (dot(source_all, qkv_weight) + qkv_bias).astype(bf16)
    attended = []
    steps = length // BQ
    marks = [0, (3 * steps + 7) // 8, (6 * steps + 7) // 8, steps]
    for p in range(3):
        attended.append(attend(qkv, marks[p], marks[p + 1] - marks[p], seg_row, seg_col, lo, hi))
    mixed_all = jnp.concatenate([a[0] for a in attended], axis=0)
    log_sums = jnp.concatenate([a[1] for a in attended], axis=1)
    mixed_heads = pick(mixed_all.reshape(-1, 2, 2, local, half), rank, 0)
    got = swap(pick(mixed_heads, 1 - c, 1), core).reshape(2 * local, half)
    kept = pick(mixed_heads, c, 1).reshape(2 * local, half)
    weight_kept = lax.dynamic_slice_in_dim(output_weight, c * half, half, 0)
    weight_got = lax.dynamic_slice_in_dim(output_weight, (1 - c) * half, half, 0)

    pre = source.astype(f32) + dot(kept, weight_kept) + dot(got, weight_got) + output_bias
    first_unit, first_inverse = norm_stats(pre)
    first = first_unit * first_gain + first_shift
    first_low = first.astype(bf16)
    inner = dot(first_low, inner_weight) + inner_bias
    phi = 0.5 * (1.0 + lax.erf(inner * math.sqrt(0.5)))
    active = (inner * phi).astype(bf16)
    slope = (phi + inner * (jnp.exp(-0.5 * inner * inner) * (1.0 / math.sqrt(2.0 * math.pi)))).astype(bf16)
    total = first + dot(active, outer_weight) + outer_bias
    second_unit, second_inverse = norm_stats(total)
    result = (second_unit * second_gain + second_shift).astype(bf16).reshape(2, local, width)

    def to_owner(values):
        stays = pick(values, y, 0)
        return in_order(y, stays, swap(pick(values, 1 - y, 0).astype(bf16), partner).astype(stays.dtype))

    layer_output = to_owner(result)

    grad = to_chip(cotangent).reshape(2 * local, width).astype(f32)
    d_total = norm_back(grad, second_gain, second_unit, second_inverse)
    d_second_gain = jnp.sum(grad * second_unit, axis=0)
    d_second_shift = jnp.sum(grad, axis=0)
    d_outer = d_total.astype(bf16)

    def over_core(gradient):
        gradient = gradient.astype(bf16)
        rows, cols = gradient.shape
        shaped = gradient.reshape(blocks + (2, rows // (2 * math.prod(blocks)), cols))
        dim = len(wanted)
        got = swap(pick(shaped, 1 - c, dim), core)
        return (pick(shaped, c, dim).astype(f32) + got.astype(f32)).astype(bf16)

    back = list(reversed(far))
    g_outer_weight = shrink(over_core(dot_rows(active, d_outer)), [near] + y_names + back, wanted)
    d_inner = (dot_cols(d_outer, outer_weight) * slope.astype(f32)).astype(bf16)
    g_inner = dot_rows(first_low, d_inner)
    g_inner = over_core(g_inner)
    d_first = dot_cols(d_inner, inner_weight) + d_total
    d_pre = norm_back(d_first, first_gain, first_unit, first_inverse)
    d_attended = d_pre.astype(bf16)
    back_got = dot_cols(d_attended, weight_got).astype(bf16).reshape(2, local, half)
    back_got = swap(back_got, core)
    back_kept = dot_cols(d_attended, weight_kept).astype(bf16).reshape(2, local, half)
    d_heads = in_order(c, back_kept, back_got, 1)
    d_heads = grow(d_heads, reversed(team)).reshape(length, half)

    g_columns = jnp.stack(
        [
            column_sums(d_attended),
            jnp.sum(d_first * first_unit, axis=0),
            jnp.sum(d_first, axis=0),
            column_sums(d_outer),
            d_second_gain,
            d_second_shift,
        ],
        axis=1,
    )
    g_columns = jnp.concatenate([g_columns, column_sums(d_inner).reshape(width, chunks)], axis=1)
    g_columns = jnp.pad(g_columns, ((0, 0), (0, PAIR - g_columns.shape[1])))
    g_output = in_order(c, dot_rows(kept, d_attended).astype(bf16), dot_rows(got, d_attended).astype(bf16))
    g_output = g_output.reshape(width, width)
    g_columns = g_columns.astype(bf16)
    g_output = over_core(jnp.concatenate([g_output, g_columns], axis=1))
    g_both = shrink(jnp.concatenate([g_inner, g_output], axis=-1), y_names + [near] + back, wanted)
    g_inner_weight, g_output = g_both[:, :hidden], g_both[:, hidden:]

    part = attend_back(qkv, 0, steps // 2, (), mixed_all, d_heads, log_sums, seg_row, seg_col, lo, hi)
    rest = attend_back(
        qkv, steps // 2, steps - steps // 2, part[1:], mixed_all, d_heads, log_sums, seg_row, seg_col, lo, hi
    )
    d_qkv = jnp.concatenate([jnp.concatenate([part[0], rest[0]], axis=0), rest[1], rest[2]], axis=1)
    place = lambda part: lax.dynamic_update_slice_in_dim(
        jnp.zeros((width,), f32), column_sums(d_qkv[:, part * half : (part + 1) * half]), c * half, 0
    )
    g_bias = jnp.pad(jnp.stack([place(0), place(2)], axis=1), ((0, 0), (0, PAIR - 2)))
    g_qkv = dot_rows(source_all, d_qkv)
    g_qkv = jnp.concatenate([g_qkv, g_bias], axis=1).astype(bf16)
    if team:
        g_qkv = jnp.where(rank == 0, g_qkv, jnp.zeros_like(g_qkv))
    g_qkv = g_qkv.reshape(blocks + (2 * own, 3 * half + PAIR))
    g_a = shrink(g_qkv[..., :cut], y_names + [near] + back, wanted)
    g_b = shrink(g_qkv[..., cut:], [near] + y_names + back, wanted)
    g_chip = jnp.concatenate([g_a, g_b], axis=1).reshape(2, own, 3 * half + PAIR)
    chip_kept = pick(g_chip, c, 0)
    chip_got = swap(pick(g_chip, 1 - c, 0), core)
    g_weights = in_order(c, chip_kept[:, : 3 * half], chip_got[:, : 3 * half])
    g_biases = chip_kept[:, 3 * half :] + chip_got[:, 3 * half :]
    g_three = [
        jnp.concatenate([g_weights[0, :, k * half : (k + 1) * half], g_weights[1, :, k * half : (k + 1) * half]], axis=1)
        for k in range(3)
    ]

    shaped = pick(d_qkv.reshape(-1, 2, 2, local, 3 * half), rank, 0)
    other = dot_cols(pick(shaped, 1 - c, 1).reshape(2 * local, 3 * half), qkv_weight).astype(bf16)
    other = swap(other, core)
    d_input = d_pre + dot_cols(pick(shaped, c, 1).reshape(2 * local, 3 * half), qkv_weight) + other.astype(f32)
    input_gradient = to_owner(d_input.reshape(2, local, width))

    return (
        layer_output,
        input_gradient,
        g_three[0],
        g_biases[:, 0],
        g_three[1],
        g_three[2],
        g_biases[:, 1],
        g_output[:, :width],
        g_output[:, width],
        g_output[:, width + 1],
        g_output[:, width + 2],
        g_inner_weight,
        g_output[:, width + 6 : width + 6 + chunks].reshape(own * chunks),
        g_outer_weight,
        g_output[:, width + 3],
        g_output[:, width + 4],
        g_output[:, width + 5],
    )


def solution(mesh):
    dp, ctx = mesh.shape["dp"], mesh.shape["ctx"]
    split = Mesh(mesh.devices.reshape(dp, ctx // 2, 2), ("dp", "y", "c"))
    every = ("dp", "y", "c")
    tokens = P("dp", ("y", "c"), None)
    matrix = P(every, None)
    vector = P(every)

    return jax.shard_map(
        on_device,
        mesh=split,
        in_specs=(
            tokens, P("dp", None), tokens,
            matrix, vector, matrix, matrix, vector, matrix, vector, vector, vector,
            matrix, vector, matrix, vector, vector, vector,
        ),
        out_specs=(
            tokens, tokens,
            matrix, vector, matrix, matrix, vector, matrix, vector, vector, vector,
            matrix, vector, matrix, vector, vector, vector,
        ),
        check_vma=False,
    )
```
